1024 devices in a mesh: pipe: 32 (over z_hi, y, core), tensor: 8 (over z_lo), dp: 4 (over x).
Axes of the slice: x: 4, y: 8, z: 16 (z_hi: 2, z_lo: 8; z = z_hi * 8 + z_lo), core: 2. Of those that a mesh axis runs over, the one named last changes fastest.
Arguments:
- narrowing_projection_weights: bfloat16 [32, 4, 5120, 256], P('pipe', None, 'tensor'), may hold values from -0.078125 to 0.078125
- widening_projection_weights: bfloat16 [32, 4, 256, 5120], P('pipe', None, None, 'tensor'), may hold values from -0.375 to 0.375
- scaling_multipliers: float32 [32, 4, 5120], P('pipe', None, 'tensor'), may hold values from 0.5 to 1.5
- slot_entry_activation: bfloat16 [32, 4, 128, 5120], P('pipe', None, 'dp', 'tensor'), may hold values from -15 to 15
- retained_section_entries: bfloat16 [2, 32, 4, 128, 5120], P(None, 'pipe', None, 'dp', 'tensor'), may hold values from -15 to 15
- slot_result_sensitivity: bfloat16 [32, 4, 128, 5120], P('pipe', None, 'dp', 'tensor'), may hold values from -4 to 4
- fresh_micro_batches: bfloat16 [1, 2, 128, 5120], P(None, None, 'dp', 'tensor'), may hold values from -15 to 15
- latest_result_sensitivity: bfloat16 [1, 2, 128, 5120], P(None, None, 'dp', 'tensor'), may hold values from -4 to 4
Outputs:
- section_outputs: bfloat16 [32, 4, 128, 5120], P('pipe', None, 'dp', 'tensor')
- input_grads: bfloat16 [32, 4, 128, 5120], P('pipe', None, 'dp', 'tensor')
- grad_down: float32 [32, 2, 5120, 256], P('pipe', None, ('tensor', 'dp'))
- grad_up: float32 [32, 2, 256, 5120], P('pipe', None, 'dp', 'tensor')
The draws below stay inside these ranges and needn't reach their ends.
All inputs are finite; a program needn't handle non-finite values.
Results may differ from the reference program's by a relative error of at most 0.025.
Values may be sent and summed in bfloat16 or wider, within the bound.
A program may use at most 32 MiB of HBM per device.

```python
import math
import jax
import jax.numpy as jnp
from jax import lax

D = 5120
R = 256
TOK = 32
TICKS = 2
SECTIONS = 64
ROWS = 128
N_PIPE = 32
N_DP = 4


def scaled_field(key, shape):
    base_key, row_key, col_key = jax.random.split(key, 3)
    base_draw = jax.random.truncated_normal(base_key, -3.0, 3.0, shape, jnp.float32)
    row_scale = jnp.exp(jax.random.uniform(row_key, shape[:-1] + (1,), jnp.float32, math.log(0.2), math.log(2.0)))
    col_scale = jnp.exp(jax.random.uniform(col_key, (shape[-1],), jnp.float32, math.log(0.7), math.log(1.4)))
    position = (jnp.arange(shape[-1], dtype=jnp.float32) + 0.5) / shape[-1] - 0.5
    ramp_scale = jnp.exp(math.log(3.0) * position)
    return (base_draw * row_scale * col_scale * ramp_scale).astype(jnp.bfloat16)


def draw_slot_entry_activation(key, part):
    return scaled_field(jax.random.fold_in(key, 11), (SECTIONS // 2, 4, ROWS, D))


def draw_retained_section_entries(key, part):
    return scaled_field(jax.random.fold_in(key, 12), (TICKS, SECTIONS // 2, 4, ROWS, D))


def draw_fresh_micro_batches(key, part):
    return scaled_field(jax.random.fold_in(key, 13), (TICKS - 1, 2, ROWS, D))


def block_scale(key, dims, shards, low, top_value):
    def one(dim, shards_of):
        steps = jax.random.uniform(jax.random.fold_in(jax.random.fold_in(key, 6), dim), (shards_of,), jnp.float32, low / len(shards), top_value / len(shards))
        return jnp.repeat(jnp.exp(steps), dims[dim] // shards_of).reshape((-1,) + (1,) * (len(dims) - dim - 1))

    level = one(*shards[0])
    for cut in shards[1:]:
        level = level * one(*cut)
    return level


def bell_draw(stream_key, extent, deviation, most, pieces=(), held_as=jnp.bfloat16):
    factor_of = block_scale(stream_key, extent, pieces, -0.22, 0.18) if pieces else 1.0
    array = jax.random.normal(stream_key, extent, jnp.float32) * deviation * factor_of
    return jnp.minimum(jnp.maximum(array, -most), most).astype(held_as)


def setup_inputs(seed: int = 0) -> dict:
    keys = jax.random.split(jax.random.key(seed), 9)
    narrowing_projection_weights = bell_draw(keys[0], (SECTIONS // 2, 4, D, R), D ** -0.5, 0.078125, ((0, 32), (2, 8)))
    widening_projection_weights = bell_draw(keys[1], (SECTIONS // 2, 4, R, D), R ** -0.5, 0.375, ((0, 32), (3, 8)))
    scaling_multipliers = jnp.clip(1.0 + 0.1 * jax.random.normal(keys[2], (SECTIONS // 2, 4, D), jnp.float32), 0.5, 1.5)
    slot_entry_activation = draw_slot_entry_activation(jax.random.fold_in(keys[8], 71), 0)
    retained_section_entries = draw_retained_section_entries(jax.random.fold_in(keys[8], 71), 0)
    slot_result_sensitivity = bell_draw(keys[5], (SECTIONS // 2, 4, ROWS, D), 1.0, 4.0, ((0, 32), (2, 4), (3, 8)))
    fresh_micro_batches = draw_fresh_micro_batches(jax.random.fold_in(keys[8], 71), 0)
    latest_result_sensitivity = bell_draw(keys[7], (TICKS - 1, 2, ROWS, D), 1.0, 4.0, ((2, 4), (3, 8)))
    return {"narrowing_projection_weights": narrowing_projection_weights, "widening_projection_weights": widening_projection_weights, "scaling_multipliers": scaling_multipliers, "slot_entry_activation": slot_entry_activation, "retained_section_entries": retained_section_entries, "slot_result_sensitivity": slot_result_sensitivity, "fresh_micro_batches": fresh_micro_batches, "latest_result_sensitivity": latest_result_sensitivity}


eps = 1e-06

def prepare(rows, gain_row, w_down):
    widened = rows.astype(jnp.float32)
    scaled = (widened * gain_row[None, :]).astype(jnp.bfloat16)
    squares = lax.optimization_barrier(jnp.sum(widened * widened, axis=-1))
    latent = jnp.dot(scaled, w_down, preferred_element_type=jnp.float32)
    factor = 1.0 / jnp.sqrt(squares / D + eps)
    preact = latent * factor[:, None]
    active = jax.nn.silu(preact).astype(jnp.bfloat16)
    return (widened, scaled, latent, factor, preact, active)

def forward(rows, gain_row, w_down, w_up):
    widened, scaled, latent, factor, preact, active = prepare(rows, gain_row, w_down)
    return (widened + jnp.dot(active, w_up, preferred_element_type=jnp.float32)).astype(jnp.bfloat16)

def backward(rows, cotangent, gain_row, w_down, w_up):
    widened, scaled, latent, factor, preact, active = prepare(rows, gain_row, w_down)
    hidden_rank_gradient = jnp.dot(cotangent, w_up.T, preferred_element_type=jnp.float32)
    sigmoid_z = jax.nn.sigmoid(preact)
    preact_grad = hidden_rank_gradient * sigmoid_z * (1.0 + preact * (1.0 - sigmoid_z))
    latent_step = (preact_grad * factor[:, None]).astype(jnp.bfloat16)
    gradient_squares = -0.5 * factor ** 3 / D * lax.optimization_barrier(jnp.sum(preact_grad * latent, axis=-1))
    feature_grad = jnp.dot(latent_step, w_down.T, preferred_element_type=jnp.float32) * gain_row[None, :]
    rows_grad = (feature_grad + 2.0 * widened * gradient_squares[:, None] + cotangent.astype(jnp.float32)).astype(jnp.bfloat16)
    return (scaled, active, latent_step, rows_grad)

def holder_tick(operands):
    entry_activation_lines, stashed, upstream, w_down, w_up, gain_rows = operands
    result_activation_lines = jax.vmap(forward)(entry_activation_lines, gain_rows, w_down, w_up)
    rows_grad = jax.vmap(backward)(stashed, upstream, gain_rows, w_down, w_up)[3]
    return (result_activation_lines, rows_grad)

def slot_terms(rows_ticks, cot_ticks, gain_row, w_down, w_up):
    down_sum = jnp.zeros((N_DP, D, R), jnp.float32)
    up_sum = jnp.zeros((N_DP, R, D), jnp.float32)
    for tick_index in range(TICKS):
        scaled, active, latent_step, unused_grad = backward(rows_ticks[tick_index], cot_ticks[tick_index], gain_row, w_down, w_up)
        scaled_groups = scaled.reshape(N_DP, TOK, D).astype(jnp.float32)
        step_groups = latent_step.reshape(N_DP, TOK, R).astype(jnp.float32)
        active_groups = active.reshape(N_DP, TOK, R).astype(jnp.float32)
        cot_groups = cot_ticks[tick_index].reshape(N_DP, TOK, D).astype(jnp.float32)
        down_sum = down_sum + jnp.einsum('gnd,gnr->gdr', scaled_groups, step_groups)
        up_sum = up_sum + jnp.einsum('gnr,gnd->grd', active_groups, cot_groups)
    down_sum = lax.optimization_barrier(down_sum.astype(jnp.bfloat16)).astype(jnp.float32)
    up_sum = lax.optimization_barrier(up_sum.astype(jnp.bfloat16)).astype(jnp.float32)
    return (lax.optimization_barrier(jnp.sum(down_sum, axis=0)), lax.optimization_barrier(jnp.sum(up_sum, axis=0)))

def reference(narrowing_projection_weights, widening_projection_weights, scaling_multipliers, slot_entry_activation, retained_section_entries, slot_result_sensitivity, fresh_micro_batches, latest_result_sensitivity):
    entry_activation_lines = slot_entry_activation
    upstream = slot_result_sensitivity
    history = []
    result_activation_lines = slot_entry_activation
    rows_grad = slot_result_sensitivity
    for tick_index in range(TICKS):
        history.append(upstream)
        result_activation_lines, rows_grad = lax.map(holder_tick, (entry_activation_lines, retained_section_entries[tick_index], upstream, narrowing_projection_weights, widening_projection_weights, scaling_multipliers))
        if tick_index + 1 < TICKS:
            entering = fresh_micro_batches[tick_index]
            arriving = latest_result_sensitivity[tick_index]
            entry_activation_lines = jnp.stack([jnp.concatenate([entering[0][None], result_activation_lines[:-1, 0]], axis=0), jnp.concatenate([result_activation_lines[1:, 1], result_activation_lines[-1:, 0]], axis=0), jnp.concatenate([result_activation_lines[1:, 2], entering[1][None]], axis=0), jnp.concatenate([result_activation_lines[:1, 2], result_activation_lines[:-1, 3]], axis=0)], axis=1)
            upstream = jnp.stack([jnp.concatenate([rows_grad[1:, 0], rows_grad[-1:, 1]], axis=0), jnp.concatenate([arriving[0][None], rows_grad[:-1, 1]], axis=0), jnp.concatenate([rows_grad[:1, 3], rows_grad[:-1, 2]], axis=0), jnp.concatenate([rows_grad[1:, 3], arriving[1][None]], axis=0)], axis=1)
    cot_history = jnp.stack(history)

    def holder_grads(holder):
        mirror_index = (N_PIPE - 1 - holder).astype(jnp.int32)
        results_down = []
        results_up = []
        for position_index in range(2):
            pairs = ((holder, position_index), (mirror_index, position_index + 2))
            total_down = jnp.zeros((D, R), jnp.float32)
            total_up = jnp.zeros((R, D), jnp.float32)
            for owner, which in pairs:
                rows_ticks = lax.dynamic_index_in_dim(retained_section_entries, owner, 1, keepdims=False)[:, which]
                cot_ticks = lax.dynamic_index_in_dim(cot_history, owner, 1, keepdims=False)[:, which]
                gain_row = lax.dynamic_index_in_dim(scaling_multipliers, owner, 0, keepdims=False)[which]
                w_down = lax.dynamic_index_in_dim(narrowing_projection_weights, owner, 0, keepdims=False)[which]
                w_up = lax.dynamic_index_in_dim(widening_projection_weights, owner, 0, keepdims=False)[which]
                term_down, term_up = slot_terms(rows_ticks, cot_ticks, gain_row, w_down, w_up)
                total_down = total_down + term_down
                total_up = total_up + term_up
            results_down.append(total_down)
            results_up.append(total_up)
        return (jnp.stack(results_down), jnp.stack(results_up))
    grad_down, grad_up = lax.map(holder_grads, jnp.arange(N_PIPE, dtype=jnp.int32))
    return (result_activation_lines, rows_grad, grad_down, grad_up)
```

```python
import functools

import jax
import jax.numpy as jnp
from jax import lax
from jax.experimental import pallas as pl
from jax.experimental.pallas import tpu as pltpu
from jax.sharding import PartitionSpec as P

MESH = pl.DeviceIdType.MESH
EPS = 1e-06
F32 = jnp.float32
BF16 = jnp.bfloat16

RS1, RS1B, AG1, AG1B, RS2, AG2 = 0, 8, 16, 24, 32, 40
UP, DOWN = 48, 52
XHG, XDY0, XDY1, XA, XDU0, XDU1 = 56, 60, 64, 68, 76, 80
MIRROR = 84
N_SEMS = 86


def nt(a, b):
    return lax.dot_general(a, b, (((1,), (1,)), ((), ())), preferred_element_type=F32)


def tn(a, b):
    return lax.dot_general(a, b, (((0,), (0,)), ((), ())), preferred_element_type=F32)


def nn(a, b):
    return jnp.dot(a, b, preferred_element_type=F32)


def lanes_of(rows, *columns):
    lane = lax.broadcasted_iota(jnp.int32, (rows, 128), 1)
    out = jnp.zeros((rows, 128), F32)
    for i, column in enumerate(columns):
        out = jnp.where(lane == i, column, out)
    return out.astype(BF16)


def kernel(
    n_pipe, n_tensor, n_dp, d_model,
    wd_hbm, wu_hbm, g_hbm, x_hbm, h_hbm, dy_hbm, fresh_hbm, latest_hbm,
    y_out, dh_out, gd_out, gu_out,
    wd, wu, g, x0, h, dy0, fresh, latest,
    hg, s1, r1, s1b, r1b, a1, a1b, s2, r2, a2, ys, ds, x1, dy1,
    hgr, dyr, ar, dur, gd, gu, msd, msu, mrd, mru, y1, dh1, god, gou,
    in_sem, own_sem, out_sem, send_sem, recv_sem,
):
    p = lax.axis_index("pipe")
    t = lax.axis_index("tensor")
    k = lax.axis_index("dp")
    last = n_pipe - 1
    slots, rows, width = x0.shape
    rank = wd.shape[2]
    half = rows // 2
    not_first, not_last = p > 0, p < last
    mirror = last - p

    barrier = pltpu.get_barrier_semaphore()

    def greet(**where):
        pl.semaphore_signal(barrier, inc=1, device_id=where, device_id_type=MESH)

    greet(pipe=mirror)
    for j in range(1, n_tensor):
        greet(tensor=lax.rem(t + j, n_tensor))

    @pl.when(not_first)
    def _():
        greet(pipe=p - 1)

    @pl.when(not_last)
    def _():
        greet(pipe=p + 1)

    for j in range(1, n_dp):
        greet(dp=lax.rem(k + j, n_dp))

    loads = {}
    for i, (name, src, dst) in enumerate([
        ("x", x_hbm.at[0], x0), ("h0", h_hbm.at[0, 0], h.at[0]), ("h1", h_hbm.at[1, 0], h.at[1]),
        ("g", g_hbm.at[0], g), ("wd", wd_hbm.at[0], wd), ("dy", dy_hbm.at[0], dy0),
        ("wu", wu_hbm.at[0], wu), ("fresh", fresh_hbm.at[0], fresh), ("latest", latest_hbm.at[0], latest),
    ]):
        loads[name] = pltpu.make_async_copy(src, dst, in_sem.at[i])
        loads[name].start()

    pending = []

    def send(src, dst, index, **where):
        copy = pltpu.make_async_remote_copy(
            src_ref=src, dst_ref=dst, send_sem=send_sem.at[index], recv_sem=recv_sem.at[index],
            device_id=where, device_id_type=MESH,
        )
        copy.start()
        return copy

    def to_peers(base, axis, src_of, dst, steps):
        me, count = {"tensor": (t, n_tensor), "dp": (k, n_dp)}[axis]
        copies = []
        for j in steps:
            peer = lax.rem(me + j, count)
            copies.append(send(src_of(peer), dst, base + j, **{axis: peer}))
        pending.extend(copies)
        return copies

    ring = [4, 3, 5, 2, 6, 1, 7] if n_tensor == 8 else list(range(1, n_tensor))
    near = list(range(1, n_dp))

    for name in ("x", "h0", "h1", "g", "wd", "dy", "wu"):
        loads[name].wait()
    for s in range(slots):
        gain = g[s : s + 1, :]
        xf, h0f, h1f = x0[s].astype(F32), h[0, s].astype(F32), h[1, s].astype(F32)
        h0s, h1s = (h0f * gain).astype(BF16), (h1f * gain).astype(BF16)
        hg[s, 0:rows] = h0s
        hg[s, rows : 2 * rows] = h1s
        stacked = jnp.concatenate([(xf * gain).astype(BF16), h0s, h1s], axis=0)
        part = nn(stacked, wd[s]).astype(BF16)
        grad = nt(dy0[s], wu[s]).astype(BF16)
        sums = [jnp.sum(v * v, axis=1, keepdims=True) for v in (xf, h0f, h1f)]
        squares = lanes_of(rows, *sums)
        for i in range(2):
            lo, hi = i * half, (i + 1) * half
            r = 2 * s + i
            s1[r, :, 0:rank] = part[lo:hi]
            s1[r, :, rank : 2 * rank] = part[rows + lo : rows + hi]
            s1[r, :, 2 * rank : 3 * rank] = grad[lo:hi]
            s1[r, :, 3 * rank : 3 * rank + 128] = squares[lo:hi]
            s1b[r] = part[2 * rows + lo : 2 * rows + hi]

    pl.semaphore_wait(barrier, n_tensor - 1 + n_dp - 1 + 1 + not_first.astype(jnp.int32) + not_last.astype(jnp.int32))

    rs1 = to_peers(RS1, "tensor", lambda peer: s1.at[peer], r1.at[t], ring)
    rs1b = to_peers(RS1B, "tensor", lambda peer: s1b.at[peer], r1b.at[t], ring)

    def window(peer):
        return hg.at[:, :, pl.ds(pl.multiple_of(peer * 128, 128), 256)]

    xhg = to_peers(XHG, "dp", window, hgr.at[k], near)
    xdy0 = to_peers(XDY0, "dp", lambda peer: dy0, dyr.at[k, 0], near)
    own_hg = pltpu.make_async_copy(window(k), hgr.at[k], own_sem.at[0])
    own_hg.start()
    dyr[k, 0] = dy0[...]

    total = s1[t].astype(F32)
    for i, copy in enumerate(rs1):
        copy.wait_recv()
        total = total + r1[lax.rem(t + n_tensor - ring[i], n_tensor)].astype(F32)

    def factor_of(column):
        return 1.0 / jnp.sqrt(column / d_model + EPS)

    fx = factor_of(total[:, 3 * rank : 3 * rank + 1])
    f0 = factor_of(total[:, 3 * rank + 1 : 3 * rank + 2])
    f1 = factor_of(total[:, 3 * rank + 2 : 3 * rank + 3])

    def back(latent, factor, da):
        z = latent * factor
        sig = jax.nn.sigmoid(z)
        dz = da * sig * (1.0 + z * (1.0 - sig))
        dss = -0.5 * factor * factor * factor / d_model * jnp.sum(dz * latent, axis=1, keepdims=True)
        high = dss.astype(BF16).astype(F32)
        return (z * sig).astype(BF16), (dz * factor).astype(BF16), lanes_of(half, high, dss - high)

    def swish(z):
        return (z * jax.nn.sigmoid(z)).astype(BF16)

    ah0, du0, dss0 = back(total[:, rank : 2 * rank], f0, total[:, 2 * rank : 3 * rank])
    a1[t, :, 0:rank] = swish(total[:, 0:rank] * fx)
    a1[t, :, rank : 2 * rank] = du0
    a1[t, :, 2 * rank : 2 * rank + 128] = dss0
    ag1 = to_peers(AG1, "tensor", lambda peer: a1.at[t], a1.at[t], ring)
    u1 = s1b[t].astype(F32)
    for i, copy in enumerate(rs1b):
        copy.wait_recv()
        u1 = u1 + r1b[lax.rem(t + n_tensor - ring[i], n_tensor)].astype(F32)
    a1b[t, :, 0:rank] = ah0
    a1b[t, :, rank : 2 * rank] = swish(u1 * f1)
    ag1b = to_peers(AG1B, "tensor", lambda peer: a1b.at[t], a1b.at[t], ring)

    def gathered(ref, s, lo, hi):
        return jnp.concatenate([ref[2 * s, :, lo:hi], ref[2 * s + 1, :, lo:hi]], axis=0)

    def outputs(ref, s, rows_in, kept, cot):
        act = gathered(ref, s, 0, rank)
        du = gathered(ref, s, rank, 2 * rank)
        pair = gathered(ref, s, 2 * rank, 2 * rank + 128).astype(F32)
        dss = pair[:, 0:1] + pair[:, 1:2]
        y = (rows_in.astype(F32) + nn(act, wu[s])).astype(BF16)
        feature = nt(du, wd[s]) * g[s : s + 1, :]
        dh = (feature + 2.0 * kept.astype(F32) * dss + cot.astype(F32)).astype(BF16)
        return y, dh

    loads["fresh"].wait()
    loads["latest"].wait()

    @pl.when(jnp.logical_not(not_first))
    def _():
        x1[0] = fresh[0]
        dy1[1] = latest[0]

    @pl.when(jnp.logical_not(not_last))
    def _():
        x1[2] = fresh[1]
        dy1[3] = latest[1]

    for copy in ag1:
        copy.wait_recv()

    def upward(s, up):
        src, dst = (ys, x1) if up else (ds, dy1)
        return src.at[s], dst.at[s]

    y_up = [True, False, False, True]
    up_index = {("y", 0): 0, ("y", 3): 1, ("d", 1): 2, ("d", 2): 3}
    down_index = {("y", 1): 0, ("y", 2): 1, ("d", 0): 2, ("d", 3): 3}

    def shift(kind, s):
        src, dst = (ys.at[s], x1.at[s]) if kind == "y" else (ds.at[s], dy1.at[s])
        if (kind, s) in up_index:
            return not_last, not_first, UP + up_index[kind, s], p + 1, src, dst
        return not_first, not_last, DOWN + down_index[kind, s], p - 1, src, dst

    def shift_copy(kind, s):
        can_send, can_receive, index, peer, src, dst = shift(kind, s)
        return can_send, can_receive, pltpu.make_async_remote_copy(
            src_ref=src, dst_ref=dst, send_sem=send_sem.at[index], recv_sem=recv_sem.at[index],
            device_id={"pipe": peer}, device_id_type=MESH,
        )

    def start_shift(kind, s):
        can_send, _, copy = shift_copy(kind, s)

        @pl.when(can_send)
        def _():
            copy.start()

    def land(kind, s):
        _, can_receive, copy = shift_copy(kind, s)

        @pl.when(can_receive)
        def _():
            copy.wait_recv()

    def drain(kind, s):
        can_send, _, copy = shift_copy(kind, s)

        @pl.when(can_send)
        def _():
            copy.wait_send()

    for s in range(slots):
        y, dh = outputs(a1, s, x0[s], h[0, s], dy0[s])
        ys[s] = y
        ds[s] = dh
        start_shift("y", s)
        start_shift("d", s)

    @pl.when(jnp.logical_not(not_first))
    def _():
        x1[3] = ys[2]
        dy1[2] = ds[3]

    @pl.when(jnp.logical_not(not_last))
    def _():
        x1[1] = ys[0]
        dy1[0] = ds[1]

    xdu0 = to_peers(XDU0, "dp", lambda peer: a1.at[:, :, rank : 2 * rank], dur.at[k, 0], near)
    dur[k, 0] = a1[:, :, rank : 2 * rank]
    for copy in ag1b:
        copy.wait_recv()

    def latents(peer, tick):
        start = pl.multiple_of(tick * rank + peer // 2 * 128, 128)
        return a1b.at[:, :, pl.ds(start, 128)]

    xa = [
        to_peers(XA + 4 * tick, "dp", functools.partial(latents, tick=tick), ar.at[k, tick], near)
        for tick in range(2)
    ]
    own_a = [pltpu.make_async_copy(latents(k, tick), ar.at[k, tick], own_sem.at[1 + tick]) for tick in range(2)]
    for copy in own_a:
        copy.start()

    for s in range(slots):
        land("y", s)
        land("d", s)
        gain = g[s : s + 1, :]
        xf = x1[s].astype(F32)
        part = nn((xf * gain).astype(BF16), wd[s]).astype(BF16)
        grad = nt(dy1[s], wu[s]).astype(BF16)
        squares = lanes_of(rows, jnp.sum(xf * xf, axis=1, keepdims=True))
        for i in range(2):
            lo, hi = i * half, (i + 1) * half
            r = 2 * s + i
            s2[r, :, 0:rank] = part[lo:hi]
            s2[r, :, rank : 2 * rank] = grad[lo:hi]
            s2[r, :, 2 * rank : 2 * rank + 128] = squares[lo:hi]
    rs2 = to_peers(RS2, "tensor", lambda peer: s2.at[peer], r2.at[t], ring)
    xdy1 = to_peers(XDY1, "dp", lambda peer: dy1, dyr.at[k, 1], near)
    dyr[k, 1] = dy1[...]

    total = s2[t].astype(F32)
    for i, copy in enumerate(rs2):
        copy.wait_recv()
        total = total + r2[lax.rem(t + n_tensor - ring[i], n_tensor)].astype(F32)
    fx = factor_of(total[:, 2 * rank : 2 * rank + 1])
    _, du1, dss1 = back(u1, f1, total[:, rank : 2 * rank])
    a2[t, :, 0:rank] = swish(total[:, 0:rank] * fx)
    a2[t, :, rank : 2 * rank] = du1
    a2[t, :, 2 * rank : 2 * rank + 128] = dss1
    ag2 = to_peers(AG2, "tensor", lambda peer: a2.at[t], a2.at[t], ring)

    for copy in own_a:
        copy.wait()
    for copy in xdy0 + xdy1 + xa[0] + xa[1]:
        copy.wait_recv()

    def all_rows(ref, s):
        return jnp.concatenate(
            [ref[q, tick, 2 * s + i] for q in range(n_dp) for tick in range(2) for i in range(2)], axis=0
        )

    def up_gradient(s):
        cot = jnp.concatenate([dyr[q, tick, s] for q in range(n_dp) for tick in range(2)], axis=0)
        return tn(all_rows(ar, s), cot)

    keep_up = pl.ds(pl.multiple_of(lax.rem(k, 2) * 64, 64), 64)
    for s in (2, 3, 0, 1):
        gu[s] = up_gradient(s)
        if s >= 2:
            msu[s - 2] = gu[s, keep_up, :].astype(BF16)
        if s == 3:
            mu = send(msu, mru, MIRROR, pipe=mirror)

    for copy in ag2:
        copy.wait_recv()
    xdu1 = to_peers(XDU1, "dp", lambda peer: a2.at[:, :, rank : 2 * rank], dur.at[k, 1], near)
    dur[k, 1] = a2[:, :, rank : 2 * rank]

    for s in range(slots):
        y, dh = outputs(a2, s, x1[s], h[1, s], dy1[s])
        y1[s] = y
        dh1[s] = dh
    out_y = pltpu.make_async_copy(y1, y_out.at[0], out_sem.at[0])
    out_dh = pltpu.make_async_copy(dh1, dh_out.at[0], out_sem.at[1])
    out_y.start()
    out_dh.start()

    own_hg.wait()
    for copy in xhg + xdu0 + xdu1:
        copy.wait_recv()
    keep_down = pl.ds(pl.multiple_of(k * 32, 32), width // n_dp)
    for s in (2, 3, 0, 1):
        factors = jnp.concatenate([hgr[q, s] for q in range(n_dp)], axis=0)
        gd[s] = tn(factors, all_rows(dur, s))
        if s >= 2:
            msd[s - 2] = gd[s, keep_down, :].astype(BF16)
        if s == 3:
            md = send(msd, mrd, MIRROR + 1, pipe=mirror)
    mu.wait_recv()
    for j in range(2):
        gou[j] = gu[j, keep_up, :] + mru[j].astype(F32)
    out_gu = pltpu.make_async_copy(gou, gu_out.at[0], out_sem.at[2])
    out_gu.start()
    md.wait_recv()
    for j in range(2):
        god[j] = gd[j, keep_down, :] + mrd[j].astype(F32)
    out_gd = pltpu.make_async_copy(god, gd_out.at[0], out_sem.at[3])
    out_gd.start()

    for copy in pending + [mu, md]:
        copy.wait_send()
    for s in range(slots):
        drain("y", s)
        drain("d", s)
    for copy in (out_y, out_dh, out_gu, out_gd):
        copy.wait()


def solution(mesh):
    n_pipe, n_tensor, n_dp = (mesh.shape[a] for a in ("pipe", "tensor", "dp"))

    def per_device(wd, wu, g, x, h, dy, fresh, latest):
        _, slots, width, rank = wd.shape
        rows = x.shape[2]
        half = rows // 2
        chunks = n_tensor
        any_spec = pl.BlockSpec(memory_space=pl.ANY)
        v = pltpu.VMEM
        return pl.pallas_call(
            functools.partial(kernel, n_pipe, n_tensor, n_dp, width * n_tensor),
            out_shape=(
                jax.ShapeDtypeStruct((1, slots, rows, width), BF16),
                jax.ShapeDtypeStruct((1, slots, rows, width), BF16),
                jax.ShapeDtypeStruct((1, 2, width // n_dp, rank), F32),
                jax.ShapeDtypeStruct((1, 2, rank // n_dp, width), F32),
            ),
            in_specs=[any_spec] * 8,
            out_specs=(any_spec,) * 4,
            scratch_shapes=[
                v((slots, width, rank), BF16), v((slots, rank, width), BF16), v((slots, width), F32),
                v((slots, rows, width), BF16), v((2, slots, rows, width), BF16), v((slots, rows, width), BF16),
                v((2, rows, width), BF16), v((2, rows, width), BF16),
                v((slots, 2 * rows, width), BF16),
                v((chunks, half, 3 * rank + 128), BF16), v((chunks, half, 3 * rank + 128), BF16),
                v((chunks, half, rank), BF16), v((chunks, half, rank), BF16),
                v((chunks, half, 2 * rank + 128), BF16), v((chunks, half, 2 * rank), BF16),
                v((chunks, half, 2 * rank + 128), BF16), v((chunks, half, 2 * rank + 128), BF16),
                v((chunks, half, 2 * rank + 128), BF16),
                v((slots, rows, width), BF16), v((slots, rows, width), BF16),
                v((slots, rows, width), BF16), v((slots, rows, width), BF16),
                v((n_dp, slots, 2 * rows, 256), BF16),
                v((n_dp, 2, slots, rows, width), BF16),
                v((n_dp, 2, chunks, half, 128), BF16),
                v((n_dp, 2, chunks, half, rank), BF16),
                v((slots, 256, rank), F32), v((slots, 128, width), F32),
                v((2, width // n_dp, rank), BF16), v((2, rank // n_dp, width), BF16),
                v((2, width // n_dp, rank), BF16), v((2, rank // n_dp, width), BF16),
                v((slots, rows, width), BF16), v((slots, rows, width), BF16),
                v((2, width // n_dp, rank), F32), v((2, rank // n_dp, width), F32),
                pltpu.SemaphoreType.DMA((9,)), pltpu.SemaphoreType.DMA((3,)), pltpu.SemaphoreType.DMA((4,)),
                pltpu.SemaphoreType.DMA((N_SEMS,)), pltpu.SemaphoreType.DMA((N_SEMS,)),
            ],
            compiler_params=pltpu.CompilerParams(
                collective_id=0, has_side_effects=True, vmem_limit_bytes=60 * 2**20
            ),
            name="relay_window",
        )(wd, wu, g, x, h, dy, fresh, latest)

    return jax.shard_map(
        per_device,
        mesh=mesh,
        in_specs=(
            P("pipe", None, "tensor", None),
            P("pipe", None, None, "tensor"),
            P("pipe", None, "tensor"),
            P("pipe", None, "dp", "tensor"),
            P(None, "pipe", None, "dp", "tensor"),
            P("pipe", None, "dp", "tensor"),
            P(None, None, "dp", "tensor"),
            P(None, None, "dp", "tensor"),
        ),
        out_specs=(
            P("pipe", None, "dp", "tensor"),
            P("pipe", None, "dp", "tensor"),
            P("pipe", None, ("tensor", "dp"), None),
            P("pipe", None, "dp", "tensor"),
        ),
        check_vma=False,
    )
```

```python
import functools

import jax
import jax.numpy as jnp
from jax import lax
from jax.experimental import pallas as pl
from jax.experimental.pallas import tpu as pltpu
from jax.sharding import PartitionSpec as P

MESH = pl.DeviceIdType.MESH
EPS = 1e-06
F32 = jnp.float32
BF16 = jnp.bfloat16

FAMILIES = {
    "rs1b": 8, "rs1f": 8, "rs1h": 8, "sq1": 8, "ag1b": 8, "ds1": 8, "ag1f": 8, "ag1a": 8,
    "rs2b": 8, "rs2f": 8, "sq2": 8, "ag2b": 8, "ds2": 8, "ag2f": 8, "up": 4, "down": 4,
    "hg": 4, "dy0": 4, "dy1": 16, "a": 8, "du0": 4, "du1": 4, "mirror": 3,
}
INDEX = {}
N_SEMS = 0
for _name, _count in FAMILIES.items():
    INDEX[_name] = N_SEMS
    N_SEMS += _count


def nt(a, b):
    return lax.dot_general(a, b, (((1,), (1,)), ((), ())), preferred_element_type=F32)


def tn(a, b):
    return lax.dot_general(a, b, (((0,), (0,)), ((), ())), preferred_element_type=F32)


def nn(a, b):
    return jnp.dot(a, b, preferred_element_type=F32)


def packed(*columns):
    rows = columns[0].shape[0]
    lane = lax.broadcasted_iota(jnp.int32, (rows, 128), 1)
    row = lax.broadcasted_iota(jnp.int32, (rows, 128), 0)
    out = jnp.zeros((rows, 128), F32)
    for i, column in enumerate(columns):
        out = jnp.where(lane == row + i * rows, column, out)
    return jnp.sum(out, axis=0, keepdims=True)


def unpacked(line, rows, i):
    lane = lax.broadcasted_iota(jnp.int32, (rows, 128), 1)
    row = lax.broadcasted_iota(jnp.int32, (rows, 128), 0)
    return jnp.sum(jnp.where(lane == row + i * rows, line, 0.0), axis=1, keepdims=True)


def kernel(
    n_pipe, n_tensor, n_dp, d_model,
    wd_hbm, wu_hbm, g_hbm, x_hbm, h_hbm, dy_hbm, fresh_hbm, latest_hbm,
    y_out, dh_out, gd_out, gu_out,
    wd, wu, g, x0, h, dy0, fresh, latest, hg,
    s1b, r1b, s1f, r1f, s1h, r1h, sq1, rq1, a1b, d1, a1f, a1a,
    s2b, r2b, s2f, r2f, sq2, rq2, a2b, d2, a2f,
    ys, ds, x1, dy1, hgr, dyr, ar, dur, gd, gu, msd, msu, mrd, mru,
    in_sem, own_sem, send_sem, recv_sem, ready,
):
    p = lax.axis_index("pipe")
    t = lax.axis_index("tensor")
    k = lax.axis_index("dp")
    last = n_pipe - 1
    middle = n_pipe // 2
    slots, rows, width = x0.shape
    rank = wd.shape[2]
    half = rows // 2
    not_first, not_last = p > 0, p < last
    upper = p >= middle
    lower = p < middle
    mirror = last - p

    barrier = pltpu.get_barrier_semaphore()

    def greet(**where):
        pl.semaphore_signal(barrier, inc=1, device_id=where, device_id_type=MESH)

    @pl.when(lower)
    def _():
        greet(pipe=mirror)

    for j in range(1, n_tensor):
        greet(tensor=lax.rem(t + j, n_tensor))

    @pl.when(jnp.logical_and(not_first, p != middle))
    def _():
        greet(pipe=p - 1)

    @pl.when(not_last)
    def _():
        greet(pipe=p + 1)

    for j in range(1, n_dp):
        greet(dp=lax.rem(k + j, n_dp))

    def load(i, src, dst):
        copy = pltpu.make_async_copy(src, dst, in_sem.at[i])
        copy.start()
        return copy

    order = [lax.rem(t // 2 + i, slots) for i in (2, 1, 3, 0)]
    first = [load(0, x_hbm.at[0], x0), load(1, h_hbm.at[0, 0], h.at[0]), load(2, h_hbm.at[1, 0], h.at[1]),
             load(3, g_hbm.at[0], g)]
    by_slot = []
    for i, s in enumerate(order):
        pair = [load(4 + 2 * i, wd_hbm.at[0, s], wd.at[s]), load(5 + 2 * i, wu_hbm.at[0, s], wu.at[s])]
        if i == 0:
            pair.append(load(12, dy_hbm.at[0], dy0))
        by_slot.append(pair)
    entering = [load(13, fresh_hbm.at[0], fresh), load(14, latest_hbm.at[0], latest)]

    pending = []

    def remote(src, dst, index, **where):
        return pltpu.make_async_remote_copy(
            src_ref=src, dst_ref=dst, send_sem=send_sem.at[index], recv_sem=recv_sem.at[index],
            device_id=where, device_id_type=MESH,
        )

    ring = [4, 3, 5, 2, 6, 1, 7] if n_tensor == 8 else list(range(1, n_tensor))
    near = list(range(1, n_dp))

    class Exchange:
        def __init__(self, family, axis, src_of, dst, offset=0):
            me, count, self.steps = (t, n_tensor, ring) if axis == "tensor" else (k, n_dp, near)
            self.base, self.axis, self.src_of, self.dst = INDEX[family] + offset, axis, src_of, dst
            self.me, self.count = me, count
            pending.append(self)

        def copy(self, peer, j):
            return remote(self.src_of(peer), self.dst, self.base + j, **{self.axis: peer})

        def start_to(self, peer):
            self.copy(peer, lax.rem(peer - self.me + self.count, self.count)).start()

        def start(self):
            for j in self.steps:
                self.copy(lax.rem(self.me + j, self.count), j).start()
            return self

        def received(self):
            for j in self.steps:
                self.copy(lax.rem(self.me + j, self.count), j).wait_recv()
                yield lax.rem(self.me + self.count - j, self.count)

        def receive(self):
            for _ in self.received():
                pass

        def drain(self):
            for j in self.steps:
                self.copy(lax.rem(self.me + j, self.count), j).wait_send()

    def scatter(family, src, dst):
        return Exchange(family, "tensor", lambda peer: src.at[peer], dst.at[t])

    def gather(family, ref):
        return Exchange(family, "tensor", lambda peer: ref.at[t], ref.at[t])

    def summed(exchange, src, dst):
        total = src[t].astype(F32)
        for q in exchange.received():
            total = total + dst[q].astype(F32)
        return total

    rs1b, rs1f, rs1h = scatter("rs1b", s1b, r1b), scatter("rs1f", s1f, r1f), scatter("rs1h", s1h, r1h)
    xsq1 = scatter("sq1", sq1, rq1)
    for copy in first:
        copy.wait()
    for n, s in enumerate(order):
        gain = g[pl.ds(s, 1), :]
        xf, h0f, h1f = x0[s].astype(F32), h[0, s].astype(F32), h[1, s].astype(F32)
        h0s, h1s = (h0f * gain).astype(BF16), (h1f * gain).astype(BF16)
        hg[s, 0:rows] = h0s
        hg[s, rows : 2 * rows] = h1s
        stacked = jnp.concatenate([h0s, (xf * gain).astype(BF16), h1s], axis=0)
        for copy in by_slot[n]:
            copy.wait()
        part = nn(stacked, wd[s]).astype(BF16)
        grad = nt(dy0[s], wu[s]).astype(BF16)
        sums = [jnp.sum(v * v, axis=1, keepdims=True) for v in (xf, h0f, h1f)]
        for i in range(2):
            lo, hi = i * half, (i + 1) * half
            r = 2 * s + i
            s1b[r, :, 0:rank] = part[lo:hi]
            s1b[r, :, rank : 2 * rank] = grad[lo:hi]
            s1f[r] = part[rows + lo : rows + hi]
            s1h[r] = part[2 * rows + lo : 2 * rows + hi]
            sq1[r] = packed(*[v[lo:hi] for v in sums])
        if n == 0:
            count = n_tensor - 1 + n_dp - 1 + not_first.astype(jnp.int32) + not_last.astype(jnp.int32)
            count = count + upper.astype(jnp.int32) - (p == middle - 1).astype(jnp.int32)
            pl.semaphore_wait(barrier, count)
        for peer in ([2 * s, 2 * s + 1] if n < slots - 1 else [t + 1 - 2 * lax.rem(t, 2)]):
            xsq1.start_to(peer)
            rs1b.start_to(peer)
    rs1f.start()
    rs1h.start()

    @pl.when(upper)
    def _():
        pl.semaphore_signal(ready.at[0], inc=1, device_id={"pipe": mirror}, device_id_type=MESH)

    @pl.when(p == middle)
    def _():
        pl.semaphore_signal(ready.at[1], inc=1, device_id={"pipe": p - 1}, device_id_type=MESH)

    def window(peer):
        return hg.at[:, :, pl.ds(pl.multiple_of(peer * 128, 128), 256)]

    xhg = Exchange("hg", "dp", window, hgr.at[k]).start()
    xdy0 = Exchange("dy0", "dp", lambda peer: dy0, dyr.at[k, 0]).start()
    own_hg = pltpu.make_async_copy(window(k), hgr.at[k], own_sem.at[0])
    own_hg.start()
    dyr[k, 0] = dy0[...]

    @pl.when(jnp.logical_not(not_first))
    def _():
        entering[0].wait()
        entering[1].wait()
        x1[0] = fresh[0]
        dy1[1] = latest[0]

    @pl.when(jnp.logical_not(not_last))
    def _():
        entering[0].wait()
        entering[1].wait()
        x1[2] = fresh[1]
        dy1[3] = latest[1]

    @pl.when(jnp.logical_and(not_first, not_last))
    def _():
        entering[0].wait()
        entering[1].wait()

    def factor_of(column):
        return 1.0 / jnp.sqrt(column / d_model + EPS)

    def back(latent, factor, da):
        z = latent * factor
        sig = jax.nn.sigmoid(z)
        dz = da * sig * (1.0 + z * (1.0 - sig))
        dss = -0.5 * factor * factor * factor / d_model * jnp.sum(dz * latent, axis=1, keepdims=True)
        return (z * sig).astype(BF16), (dz * factor).astype(BF16), packed(dss)

    def swish(z):
        return (z * jax.nn.sigmoid(z)).astype(BF16)

    squares = summed(xsq1, sq1, rq1)
    fx, f0, f1 = (factor_of(unpacked(squares, half, i)) for i in range(3))
    total = summed(rs1b, s1b, r1b)
    ah0, du0, dss0 = back(total[:, 0:rank], f0, total[:, rank : 2 * rank])
    a1b[t] = du0
    d1[t] = dss0
    ag1b = gather("ag1b", a1b).start()
    xds1 = gather("ds1", d1).start()
    a1f[t] = swish(summed(rs1f, s1f, r1f) * fx)
    ag1f = gather("ag1f", a1f).start()
    u1 = summed(rs1h, s1h, r1h)
    a1a[t, :, 0:rank] = ah0
    a1a[t, :, rank : 2 * rank] = swish(u1 * f1)
    ag1a = gather("ag1a", a1a).start()

    def both(ref, s):
        return jnp.concatenate([ref[2 * s], ref[2 * s + 1]], axis=0)

    def dh_of(a_ref, d_ref, s, kept, cot):
        dss = jnp.concatenate([unpacked(d_ref[2 * s + i], half, 0) for i in range(2)], axis=0)
        feature = nt(both(a_ref, s), wd[s]) * g[s : s + 1, :]
        return (feature + 2.0 * kept.astype(F32) * dss + cot.astype(F32)).astype(BF16)

    def y_of(a_ref, s, rows_in):
        return (rows_in.astype(F32) + nn(both(a_ref, s), wu[s])).astype(BF16)

    up_index = {("y", 0): 0, ("y", 3): 1, ("d", 1): 2, ("d", 2): 3}
    down_index = {("y", 1): 0, ("y", 2): 1, ("d", 0): 2, ("d", 3): 3}

    def shift(kind, s):
        src, dst = (ys.at[s], x1.at[s]) if kind == "y" else (ds.at[s], dy1.at[s])
        if (kind, s) in up_index:
            copy = remote(src, dst, INDEX["up"] + up_index[kind, s], pipe=p + 1)
            return not_last, not_first, copy
        copy = remote(src, dst, INDEX["down"] + down_index[kind, s], pipe=p - 1)
        return not_first, not_last, copy

    def start_shift(kind, s):
        can_send, _, copy = shift(kind, s)
        pl.when(can_send)(copy.start)

    def land(kind, s):
        _, can_receive, copy = shift(kind, s)
        pl.when(can_receive)(copy.wait_recv)

    def drain(kind, s):
        can_send, _, copy = shift(kind, s)
        pl.when(can_send)(copy.wait_send)

    ag1b.receive()
    xds1.receive()

    @pl.when(p == middle - 1)
    def _():
        pl.semaphore_wait(ready.at[1], 1)

    for s in (2, 3, 0, 1):
        ds[s] = dh_of(a1b, d1, s, h[0, s], dy0[s])
        start_shift("d", s)
    xdu0 = Exchange("du0", "dp", lambda peer: a1b, dur.at[k, 0]).start()
    dur[k, 0] = a1b[...]

    @pl.when(jnp.logical_not(not_first))
    def _():
        dy1[2] = ds[3]

    @pl.when(jnp.logical_not(not_last))
    def _():
        dy1[0] = ds[1]

    ag1f.receive()
    for s in range(slots):
        ys[s] = y_of(a1f, s, x0[s])
        start_shift("y", s)

    @pl.when(jnp.logical_not(not_first))
    def _():
        x1[3] = ys[2]

    @pl.when(jnp.logical_not(not_last))
    def _():
        x1[1] = ys[0]

    rs2b, rs2f = scatter("rs2b", s2b, r2b), scatter("rs2f", s2f, r2f)
    xsq2 = scatter("sq2", sq2, rq2)
    xdy1 = []
    for s in (2, 3, 0, 1):
        land("d", s)
        grad = nt(dy1[s], wu[s]).astype(BF16)
        for i in range(2):
            r = 2 * s + i
            s2b[r] = grad[i * half : (i + 1) * half]

            @pl.when(t != r)
            def _():
                rs2b.start_to(r)

        xdy1.append(Exchange("dy1", "dp", lambda peer, s=s: dy1.at[s], dyr.at[k, 1, s], 4 * s).start())
    dyr[k, 1] = dy1[...]
    for s in range(slots):
        land("y", s)
        xf = x1[s].astype(F32)
        part = nn((xf * g[s : s + 1, :]).astype(BF16), wd[s]).astype(BF16)
        squares = jnp.sum(xf * xf, axis=1, keepdims=True)
        for i in range(2):
            lo, hi = i * half, (i + 1) * half
            s2f[2 * s + i] = part[lo:hi]
            sq2[2 * s + i] = packed(squares[lo:hi])
    xsq2.start()
    rs2f.start()

    ag1a.receive()

    def latents(peer, tick):
        return a1a.at[:, :, pl.ds(pl.multiple_of(tick * rank + peer // 2 * 128, 128), 128)]

    xa = [
        Exchange("a", "dp", functools.partial(latents, tick=tick), ar.at[k, tick], 4 * tick).start()
        for tick in range(2)
    ]
    own_a = [pltpu.make_async_copy(latents(k, tick), ar.at[k, tick], own_sem.at[1 + tick]) for tick in range(2)]
    for copy in own_a:
        copy.start()

    _, du1, dss1 = back(u1, f1, summed(rs2b, s2b, r2b))
    a2b[t] = du1
    d2[t] = dss1
    ag2b = gather("ag2b", a2b).start()
    xds2 = gather("ds2", d2).start()

    for copy in own_a:
        copy.wait()
    for exchange in [xdy0] + xdy1 + xa:
        exchange.receive()

    @pl.when(lower)
    def _():
        pl.semaphore_wait(ready.at[0], 1)

    def all_rows(ref, s):
        return jnp.concatenate(
            [ref[q, tick, 2 * s + i] for q in range(n_dp) for tick in range(2) for i in range(2)], axis=0
        )

    def up_gradient(s):
        cot = jnp.concatenate([dyr[q, tick, s] for q in range(n_dp) for tick in range(2)], axis=0)
        return tn(all_rows(ar, s), cot)

    keep_up = pl.ds(pl.multiple_of(lax.rem(k, 2) * 64, 64), 64)
    for s in (2, 3):
        gu[s] = up_gradient(s)
        msu[s - 2] = gu[s, keep_up, :].astype(BF16)
    mu = remote(msu, mru, INDEX["mirror"], pipe=mirror)
    mu.start()

    ag2b.receive()
    xds2.receive()
    xdu1 = Exchange("du1", "dp", lambda peer: a2b, dur.at[k, 1]).start()
    dur[k, 1] = a2b[...]
    squares = summed(xsq2, sq2, rq2)
    a2f[t] = swish(summed(rs2f, s2f, r2f) * factor_of(unpacked(squares, half, 0)))
    ag2f = gather("ag2f", a2f).start()

    own_hg.wait()
    for exchange in (xhg, xdu0, xdu1):
        exchange.receive()
    keep_down = pl.ds(pl.multiple_of(k * 32, 32), width // n_dp)

    def down_gradient(s):
        factors = jnp.concatenate([hgr[q, s] for q in range(n_dp)], axis=0)
        return tn(factors, all_rows(dur, s))

    md = []
    for s in (2, 3):
        gd[s] = down_gradient(s)
        msd[s - 2] = gd[s, keep_down, :].astype(BF16)
        md.append(remote(msd.at[s - 2], mrd.at[s - 2], INDEX["mirror"] + s - 1, pipe=mirror))
        md[-1].start()
    for s in (0, 1):
        gu[s] = up_gradient(s)
        gd[s] = down_gradient(s)
    for s in range(slots):
        dh_out[0, s] = dh_of(a2b, d2, s, h[1, s], dy1[s])
    ag2f.receive()
    for s in range(slots):
        y_out[0, s] = y_of(a2f, s, x1[s])
    mu.wait_recv()
    for j in range(2):
        gu_out[0, j] = gu[j, keep_up, :] + mru[j].astype(F32)
    for j in range(2):
        md[j].wait_recv()
        gd_out[0, j] = gd[j, keep_down, :] + mrd[j].astype(F32)

    for exchange in pending:
        exchange.drain()
    for copy in [mu] + md:
        copy.wait_send()
    for s in range(slots):
        drain("y", s)
        drain("d", s)


def solution(mesh):
    n_pipe, n_tensor, n_dp = (mesh.shape[a] for a in ("pipe", "tensor", "dp"))

    def per_device(wd, wu, g, x, h, dy, fresh, latest):
        _, slots, width, rank = wd.shape
        rows = x.shape[2]
        half = rows // 2
        chunks = n_tensor
        any_spec = pl.BlockSpec(memory_space=pl.ANY)
        vmem_spec = pl.BlockSpec(memory_space=pltpu.VMEM)
        v = pltpu.VMEM
        shapes = [
            ((1, slots, rows, width), BF16), ((1, slots, rows, width), BF16),
            ((1, 2, width // n_dp, rank), F32), ((1, 2, rank // n_dp, width), F32),
        ]

        def chunk(columns):
            return v((chunks, half, columns), BF16)

        line = v((chunks, 1, 128), F32)
        act = v((slots, rows, width), BF16)
        results = pl.pallas_call(
            functools.partial(kernel, n_pipe, n_tensor, n_dp, width * n_tensor),
            out_shape=tuple(v(*shape) for shape in shapes),
            in_specs=[any_spec] * 8,
            out_specs=(vmem_spec,) * 4,
            scratch_shapes=[
                v((slots, width, rank), BF16), v((slots, rank, width), BF16), v((slots, width), F32),
                act, v((2, slots, rows, width), BF16), act,
                v((2, rows, width), BF16), v((2, rows, width), BF16),
                v((slots, 2 * rows, width), BF16),
                chunk(2 * rank), chunk(2 * rank), chunk(rank), chunk(rank), chunk(rank), chunk(rank),
                line, line, chunk(rank), line, chunk(rank), chunk(2 * rank),
                chunk(rank), chunk(rank), chunk(rank), chunk(rank), line, line, chunk(rank), line, chunk(rank),
                act, act, act, act,
                v((n_dp, slots, 2 * rows, 256), BF16),
                v((n_dp, 2, slots, rows, width), BF16),
                v((n_dp, 2, chunks, half, 128), BF16),
                v((n_dp, 2, chunks, half, rank), BF16),
                v((slots, 256, rank), F32), v((slots, 128, width), F32),
                v((2, width // n_dp, rank), BF16), v((2, rank // n_dp, width), BF16),
                v((2, width // n_dp, rank), BF16), v((2, rank // n_dp, width), BF16),
                pltpu.SemaphoreType.DMA((15,)), pltpu.SemaphoreType.DMA((3,)),
                pltpu.SemaphoreType.DMA((N_SEMS,)), pltpu.SemaphoreType.DMA((N_SEMS,)),
                pltpu.SemaphoreType.REGULAR((2,)),
            ],
            compiler_params=pltpu.CompilerParams(
                collective_id=0, has_side_effects=True, vmem_limit_bytes=60 * 2**20
            ),
            name="relay_window",
        )(wd, wu, g, x, h, dy, fresh, latest)
        return results

    return jax.shard_map(
        per_device,
        mesh=mesh,
        in_specs=(
            P("pipe", None, "tensor", None),
            P("pipe", None, None, "tensor"),
            P("pipe", None, "tensor"),
            P("pipe", None, "dp", "tensor"),
            P(None, "pipe", None, "dp", "tensor"),
            P("pipe", None, "dp", "tensor"),
            P(None, None, "dp", "tensor"),
            P(None, None, "dp", "tensor"),
        ),
        out_specs=(
            P("pipe", None, "dp", "tensor"),
            P("pipe", None, "dp", "tensor"),
            P("pipe", None, ("tensor", "dp"), None),
            P("pipe", None, "dp", "tensor"),
        ),
        check_vma=False,
    )
```

```python
import functools

import jax
import jax.numpy as jnp
from jax import lax
from jax.experimental import pallas as pl
from jax.experimental.pallas import tpu as pltpu
from jax.sharding import PartitionSpec as P

MESH = pl.DeviceIdType.MESH
EPS = 1e-06
F32 = jnp.float32
BF16 = jnp.bfloat16

FAMILIES = {
    "rs1b": 8, "rs1f": 8, "rs1h": 8, "sq1": 8, "ag1b": 8, "ds1": 8, "ag1f": 8, "ag1a": 8,
    "rs2b": 8, "rs2f": 8, "sq2": 8, "ag2b": 8, "ds2": 8, "ag2f": 8, "up": 4, "down": 4,
    "hg": 4, "dy0": 4, "dy1": 16, "a": 8, "du0": 4, "du1": 4, "mirror": 3,
}
INDEX = {}
N_SEMS = 0
for _name, _count in FAMILIES.items():
    INDEX[_name] = N_SEMS
    N_SEMS += _count


def nt(a, b):
    return lax.dot_general(a, b, (((1,), (1,)), ((), ())), preferred_element_type=F32)


def tn(a, b):
    return lax.dot_general(a, b, (((0,), (0,)), ((), ())), preferred_element_type=F32)


def nn(a, b):
    return jnp.dot(a, b, preferred_element_type=F32)


def packed(*columns):
    rows = columns[0].shape[0]
    lane = lax.broadcasted_iota(jnp.int32, (rows, 128), 1)
    row = lax.broadcasted_iota(jnp.int32, (rows, 128), 0)
    out = jnp.zeros((rows, 128), F32)
    for i, column in enumerate(columns):
        out = jnp.where(lane == row + i * rows, column, out)
    return jnp.sum(out, axis=0, keepdims=True)


def unpacked(line, rows, i):
    lane = lax.broadcasted_iota(jnp.int32, (rows, 128), 1)
    row = lax.broadcasted_iota(jnp.int32, (rows, 128), 0)
    return jnp.sum(jnp.where(lane == row + i * rows, line, 0.0), axis=1, keepdims=True)


def kernel(
    n_pipe, n_tensor, n_dp, d_model,
    wd_hbm, wu_hbm, g_hbm, x_hbm, h_hbm, dy_hbm, fresh_hbm, latest_hbm,
    y_out, dh_out, gd_out, gu_out,
    wd, wu, g, x0, h, dy0, fresh, latest, hg,
    s1b, r1b, s1f, r1f, s1h, r1h, sq1, rq1, a1b, d1, a1f, a1a,
    s2b, r2b, s2f, r2f, sq2, rq2, a2b, d2, a2f,
    ys, ds, x1, dy1, hgr, dyr, ar, dur, gd, gu, msd, msu, mrd, mru,
    in_sem, own_sem, send_sem, recv_sem, ready,
):
    p = lax.axis_index("pipe")
    t = lax.axis_index("tensor")
    k = lax.axis_index("dp")
    last = n_pipe - 1
    middle = n_pipe // 2
    slots, rows, width = x0.shape
    rank = wd.shape[2]
    half = rows // 2
    not_first, not_last = p > 0, p < last
    upper = p >= middle
    lower = p < middle
    mirror = last - p

    barrier = pltpu.get_barrier_semaphore()

    def greet(**where):
        pl.semaphore_signal(barrier, inc=1, device_id=where, device_id_type=MESH)

    @pl.when(lower)
    def _():
        greet(pipe=mirror)

    for j in range(1, n_tensor):
        greet(tensor=lax.rem(t + j, n_tensor))

    @pl.when(jnp.logical_and(not_first, p != middle))
    def _():
        greet(pipe=p - 1)

    @pl.when(not_last)
    def _():
        greet(pipe=p + 1)

    for j in range(1, n_dp):
        greet(dp=lax.rem(k + j, n_dp))

    def load(i, src, dst):
        copy = pltpu.make_async_copy(src, dst, in_sem.at[i])
        copy.start()
        return copy

    order = [lax.rem(t // 2 + i, slots) for i in (2, 1, 3, 0)]
    first = [load(0, x_hbm.at[0], x0), load(1, h_hbm.at[0, 0], h.at[0]), load(2, h_hbm.at[1, 0], h.at[1]),
             load(3, g_hbm.at[0], g)]
    by_slot = []
    for i, s in enumerate(order):
        pair = [load(4 + 2 * i, wd_hbm.at[0, s], wd.at[s]), load(5 + 2 * i, wu_hbm.at[0, s], wu.at[s])]
        if i == 0:
            pair.append(load(12, dy_hbm.at[0], dy0))
        by_slot.append(pair)
    entering = [load(13, fresh_hbm.at[0], fresh), load(14, latest_hbm.at[0], latest)]

    pending = []

    def remote(src, dst, index, **where):
        return pltpu.make_async_remote_copy(
            src_ref=src, dst_ref=dst, send_sem=send_sem.at[index], recv_sem=recv_sem.at[index],
            device_id=where, device_id_type=MESH,
        )

    ring = [4, 3, 5, 2, 6, 1, 7] if n_tensor == 8 else list(range(1, n_tensor))
    near = list(range(1, n_dp))

    class Exchange:
        def __init__(self, family, axis, src_of, dst, offset=0):
            me, count, self.steps = (t, n_tensor, ring) if axis == "tensor" else (k, n_dp, near)
            self.base, self.axis, self.src_of, self.dst = INDEX[family] + offset, axis, src_of, dst
            self.me, self.count = me, count
            pending.append(self)

        def copy(self, peer, j):
            return remote(self.src_of(peer), self.dst, self.base + j, **{self.axis: peer})

        def start_to(self, peer):
            self.copy(peer, lax.rem(peer - self.me + self.count, self.count)).start()

        def start(self):
            for j in self.steps:
                self.copy(lax.rem(self.me + j, self.count), j).start()
            return self

        def received(self):
            for j in self.steps:
                self.copy(lax.rem(self.me + j, self.count), j).wait_recv()
                yield lax.rem(self.me + self.count - j, self.count)

        def receive(self):
            for _ in self.received():
                pass

        def drain(self):
            for j in self.steps:
                self.copy(lax.rem(self.me + j, self.count), j).wait_send()

    def scatter(family, src, dst):
        return Exchange(family, "tensor", lambda peer: src.at[peer], dst.at[t])

    def gather(family, ref):
        return Exchange(family, "tensor", lambda peer: ref.at[t], ref.at[t])

    def summed(exchange, src, dst):
        total = src[t].astype(F32)
        for q in exchange.received():
            total = total + dst[q].astype(F32)
        return total

    rs1b, rs1f, rs1h = scatter("rs1b", s1b, r1b), scatter("rs1f", s1f, r1f), scatter("rs1h", s1h, r1h)
    xsq1 = scatter("sq1", sq1, rq1)
    for copy in first:
        copy.wait()
    for n, s in enumerate(order):
        gain = g[pl.ds(s, 1), :]
        xf, h0f, h1f = x0[s].astype(F32), h[0, s].astype(F32), h[1, s].astype(F32)
        h0s, h1s = (h0f * gain).astype(BF16), (h1f * gain).astype(BF16)
        hg[s, 0:rows] = h0s
        hg[s, rows : 2 * rows] = h1s
        stacked = jnp.concatenate([h0s, (xf * gain).astype(BF16), h1s], axis=0)
        for copy in by_slot[n]:
            copy.wait()
        part = nn(stacked, wd[s]).astype(BF16)
        grad = nt(dy0[s], wu[s]).astype(BF16)
        sums = [jnp.sum(v * v, axis=1, keepdims=True) for v in (xf, h0f, h1f)]
        for i in range(2):
            lo, hi = i * half, (i + 1) * half
            r = 2 * s + i
            s1b[r, :, 0:rank] = part[lo:hi]
            s1b[r, :, rank : 2 * rank] = grad[lo:hi]
            s1f[r] = part[rows + lo : rows + hi]
            s1h[r] = part[2 * rows + lo : 2 * rows + hi]
            sq1[r] = packed(*[v[lo:hi] for v in sums])
        if n == 0:
            count = n_tensor - 1 + n_dp - 1 + not_first.astype(jnp.int32) + not_last.astype(jnp.int32)
            count = count + upper.astype(jnp.int32) - (p == middle - 1).astype(jnp.int32)
            pl.semaphore_wait(barrier, count)
        for peer in ([2 * s, 2 * s + 1] if n < slots - 1 else [t + 1 - 2 * lax.rem(t, 2)]):
            xsq1.start_to(peer)
            rs1b.start_to(peer)

    @pl.when(upper)
    def _():
        pl.semaphore_signal(ready.at[0], inc=1, device_id={"pipe": mirror}, device_id_type=MESH)

    @pl.when(p == middle)
    def _():
        pl.semaphore_signal(ready.at[1], inc=1, device_id={"pipe": p - 1}, device_id_type=MESH)

    def window(peer):
        return hg.at[:, :, pl.ds(pl.multiple_of(peer * 128, 128), 256)]

    xhg = Exchange("hg", "dp", window, hgr.at[k]).start()
    xdy0 = Exchange("dy0", "dp", lambda peer: dy0, dyr.at[k, 0]).start()
    own_hg = pltpu.make_async_copy(window(k), hgr.at[k], own_sem.at[0])
    own_hg.start()
    dyr[k, 0] = dy0[...]

    @pl.when(jnp.logical_not(not_first))
    def _():
        entering[0].wait()
        entering[1].wait()
        x1[0] = fresh[0]
        dy1[1] = latest[0]

    @pl.when(jnp.logical_not(not_last))
    def _():
        entering[0].wait()
        entering[1].wait()
        x1[2] = fresh[1]
        dy1[3] = latest[1]

    @pl.when(jnp.logical_and(not_first, not_last))
    def _():
        entering[0].wait()
        entering[1].wait()

    def factor_of(column):
        return 1.0 / jnp.sqrt(column / d_model + EPS)

    def back(latent, factor, da):
        z = latent * factor
        sig = jax.nn.sigmoid(z)
        dz = da * sig * (1.0 + z * (1.0 - sig))
        dss = -0.5 * factor * factor * factor / d_model * jnp.sum(dz * latent, axis=1, keepdims=True)
        return (z * sig).astype(BF16), (dz * factor).astype(BF16), packed(dss)

    def swish(z):
        return (z * jax.nn.sigmoid(z)).astype(BF16)

    squares = summed(xsq1, sq1, rq1)
    fx, f0, f1 = (factor_of(unpacked(squares, half, i)) for i in range(3))
    total = summed(rs1b, s1b, r1b)
    ah0, du0, dss0 = back(total[:, 0:rank], f0, total[:, rank : 2 * rank])
    a1b[t] = du0
    d1[t] = dss0
    ag1b = gather("ag1b", a1b).start()
    xds1 = gather("ds1", d1).start()
    rs1f.start()
    rs1h.start()

    def both(ref, s):
        return jnp.concatenate([ref[2 * s], ref[2 * s + 1]], axis=0)

    def dh_of(a_ref, d_ref, s, kept, cot):
        dss = jnp.concatenate([unpacked(d_ref[2 * s + i], half, 0) for i in range(2)], axis=0)
        feature = nt(both(a_ref, s), wd[s]) * g[s : s + 1, :]
        return (feature + 2.0 * kept.astype(F32) * dss + cot.astype(F32)).astype(BF16)

    def y_of(a_ref, s, rows_in):
        return (rows_in.astype(F32) + nn(both(a_ref, s), wu[s])).astype(BF16)

    up_index = {("y", 0): 0, ("y", 3): 1, ("d", 1): 2, ("d", 2): 3}
    down_index = {("y", 1): 0, ("y", 2): 1, ("d", 0): 2, ("d", 3): 3}

    def shift(kind, s):
        src, dst = (ys.at[s], x1.at[s]) if kind == "y" else (ds.at[s], dy1.at[s])
        if (kind, s) in up_index:
            copy = remote(src, dst, INDEX["up"] + up_index[kind, s], pipe=p + 1)
            return not_last, not_first, copy
        copy = remote(src, dst, INDEX["down"] + down_index[kind, s], pipe=p - 1)
        return not_first, not_last, copy

    def start_shift(kind, s):
        can_send, _, copy = shift(kind, s)
        pl.when(can_send)(copy.start)

    def land(kind, s):
        _, can_receive, copy = shift(kind, s)
        pl.when(can_receive)(copy.wait_recv)

    def drain(kind, s):
        can_send, _, copy = shift(kind, s)
        pl.when(can_send)(copy.wait_send)

    ag1b.receive()
    xds1.receive()

    @pl.when(p == middle - 1)
    def _():
        pl.semaphore_wait(ready.at[1], 1)

    for s in (2, 3, 0, 1):
        ds[s] = dh_of(a1b, d1, s, h[0, s], dy0[s])
        start_shift("d", s)
    xdu0 = Exchange("du0", "dp", lambda peer: a1b, dur.at[k, 0]).start()
    dur[k, 0] = a1b[...]

    @pl.when(jnp.logical_not(not_first))
    def _():
        dy1[2] = ds[3]

    @pl.when(jnp.logical_not(not_last))
    def _():
        dy1[0] = ds[1]

    a1f[t] = swish(summed(rs1f, s1f, r1f) * fx)
    ag1f = gather("ag1f", a1f).start()
    u1 = summed(rs1h, s1h, r1h)
    a1a[t, :, 0:rank] = ah0
    a1a[t, :, rank : 2 * rank] = swish(u1 * f1)
    ag1a = gather("ag1a", a1a).start()

    rs2b, rs2f = scatter("rs2b", s2b, r2b), scatter("rs2f", s2f, r2f)
    xsq2 = scatter("sq2", sq2, rq2)
    xdy1 = []
    for s in (2, 3, 0, 1):
        land("d", s)
        grad = nt(dy1[s], wu[s]).astype(BF16)
        for i in range(2):
            r = 2 * s + i
            s2b[r] = grad[i * half : (i + 1) * half]

            @pl.when(t != r)
            def _():
                rs2b.start_to(r)

        xdy1.append(Exchange("dy1", "dp", lambda peer, s=s: dy1.at[s], dyr.at[k, 1, s], 4 * s).start())
    dyr[k, 1] = dy1[...]
    ag1f.receive()
    for s in range(slots):
        ys[s] = y_of(a1f, s, x0[s])
        start_shift("y", s)

    @pl.when(jnp.logical_not(not_first))
    def _():
        x1[3] = ys[2]

    @pl.when(jnp.logical_not(not_last))
    def _():
        x1[1] = ys[0]

    ag1a.receive()

    def latents(peer, tick):
        return a1a.at[:, :, pl.ds(pl.multiple_of(tick * rank + peer // 2 * 128, 128), 128)]

    xa = [
        Exchange("a", "dp", functools.partial(latents, tick=tick), ar.at[k, tick], 4 * tick).start()
        for tick in range(2)
    ]
    own_a = [pltpu.make_async_copy(latents(k, tick), ar.at[k, tick], own_sem.at[1 + tick]) for tick in range(2)]
    for copy in own_a:
        copy.start()

    _, du1, dss1 = back(u1, f1, summed(rs2b, s2b, r2b))
    a2b[t] = du1
    d2[t] = dss1
    ag2b = gather("ag2b", a2b).start()
    xds2 = gather("ds2", d2).start()

    for copy in own_a:
        copy.wait()
    for exchange in [xdy0] + xdy1 + xa:
        exchange.receive()

    @pl.when(lower)
    def _():
        pl.semaphore_wait(ready.at[0], 1)

    def all_rows(ref, s):
        return jnp.concatenate(
            [ref[q, tick, 2 * s + i] for q in range(n_dp) for tick in range(2) for i in range(2)], axis=0
        )

    def up_gradient(s):
        cot = jnp.concatenate([dyr[q, tick, s] for q in range(n_dp) for tick in range(2)], axis=0)
        return tn(all_rows(ar, s), cot)

    keep_up = pl.ds(pl.multiple_of(lax.rem(k, 2) * 64, 64), 64)
    for s in (2, 3):
        gu[s] = up_gradient(s)
        msu[s - 2] = gu[s, keep_up, :].astype(BF16)
    mu = remote(msu, mru, INDEX["mirror"], pipe=mirror)
    mu.start()

    for s in range(slots):
        land("y", s)
        xf = x1[s].astype(F32)
        part = nn((xf * g[s : s + 1, :]).astype(BF16), wd[s]).astype(BF16)
        squares = jnp.sum(xf * xf, axis=1, keepdims=True)
        for i in range(2):
            lo, hi = i * half, (i + 1) * half
            s2f[2 * s + i] = part[lo:hi]
            sq2[2 * s + i] = packed(squares[lo:hi])
    xsq2.start()
    rs2f.start()

    ag2b.receive()
    xds2.receive()
    xdu1 = Exchange("du1", "dp", lambda peer: a2b, dur.at[k, 1]).start()
    dur[k, 1] = a2b[...]
    own_hg.wait()
    for exchange in (xhg, xdu0, xdu1):
        exchange.receive()
    keep_down = pl.ds(pl.multiple_of(k * 32, 32), width // n_dp)

    def down_gradient(s):
        factors = jnp.concatenate([hgr[q, s] for q in range(n_dp)], axis=0)
        return tn(factors, all_rows(dur, s))

    md = []
    for s in (2, 3):
        gd[s] = down_gradient(s)
        msd[s - 2] = gd[s, keep_down, :].astype(BF16)
        md.append(remote(msd.at[s - 2], mrd.at[s - 2], INDEX["mirror"] + s - 1, pipe=mirror))
        md[-1].start()
    squares = summed(xsq2, sq2, rq2)
    a2f[t] = swish(summed(rs2f, s2f, r2f) * factor_of(unpacked(squares, half, 0)))
    ag2f = gather("ag2f", a2f).start()
    for s in (0, 1):
        gu[s] = up_gradient(s)
        gd[s] = down_gradient(s)
    for s in range(slots):
        dh_out[0, s] = dh_of(a2b, d2, s, h[1, s], dy1[s])
    ag2f.receive()
    for s in range(slots):
        y_out[0, s] = y_of(a2f, s, x1[s])
    mu.wait_recv()
    for j in range(2):
        gu_out[0, j] = gu[j, keep_up, :] + mru[j].astype(F32)
    for j in range(2):
        md[j].wait_recv()
        gd_out[0, j] = gd[j, keep_down, :] + mrd[j].astype(F32)

    for exchange in pending:
        exchange.drain()
    for copy in [mu] + md:
        copy.wait_send()
    for s in range(slots):
        drain("y", s)
        drain("d", s)


def solution(mesh):
    n_pipe, n_tensor, n_dp = (mesh.shape[a] for a in ("pipe", "tensor", "dp"))

    def per_device(wd, wu, g, x, h, dy, fresh, latest):
        _, slots, width, rank = wd.shape
        rows = x.shape[2]
        half = rows // 2
        chunks = n_tensor
        any_spec = pl.BlockSpec(memory_space=pl.ANY)
        vmem_spec = pl.BlockSpec(memory_space=pltpu.VMEM)
        v = pltpu.VMEM
        shapes = [
            ((1, slots, rows, width), BF16), ((1, slots, rows, width), BF16),
            ((1, 2, width // n_dp, rank), F32), ((1, 2, rank // n_dp, width), F32),
        ]

        def chunk(columns):
            return v((chunks, half, columns), BF16)

        line = v((chunks, 1, 128), F32)
        act = v((slots, rows, width), BF16)
        results = pl.pallas_call(
            functools.partial(kernel, n_pipe, n_tensor, n_dp, width * n_tensor),
            out_shape=tuple(v(*shape) for shape in shapes),
            in_specs=[any_spec] * 8,
            out_specs=(vmem_spec,) * 4,
            scratch_shapes=[
                v((slots, width, rank), BF16), v((slots, rank, width), BF16), v((slots, width), F32),
                act, v((2, slots, rows, width), BF16), act,
                v((2, rows, width), BF16), v((2, rows, width), BF16),
                v((slots, 2 * rows, width), BF16),
                chunk(2 * rank), chunk(2 * rank), chunk(rank), chunk(rank), chunk(rank), chunk(rank),
                line, line, chunk(rank), line, chunk(rank), chunk(2 * rank),
                chunk(rank), chunk(rank), chunk(rank), chunk(rank), line, line, chunk(rank), line, chunk(rank),
                act, act, act, act,
                v((n_dp, slots, 2 * rows, 256), BF16),
                v((n_dp, 2, slots, rows, width), BF16),
                v((n_dp, 2, chunks, half, 128), BF16),
                v((n_dp, 2, chunks, half, rank), BF16),
                v((slots, 256, rank), F32), v((slots, 128, width), F32),
                v((2, width // n_dp, rank), BF16), v((2, rank // n_dp, width), BF16),
                v((2, width // n_dp, rank), BF16), v((2, rank // n_dp, width), BF16),
                pltpu.SemaphoreType.DMA((15,)), pltpu.SemaphoreType.DMA((3,)),
                pltpu.SemaphoreType.DMA((N_SEMS,)), pltpu.SemaphoreType.DMA((N_SEMS,)),
                pltpu.SemaphoreType.REGULAR((2,)),
            ],
            compiler_params=pltpu.CompilerParams(
                collective_id=0, has_side_effects=True, vmem_limit_bytes=60 * 2**20
            ),
            name="relay_window",
        )(wd, wu, g, x, h, dy, fresh, latest)
        return results

    return jax.shard_map(
        per_device,
        mesh=mesh,
        in_specs=(
            P("pipe", None, "tensor", None),
            P("pipe", None, None, "tensor"),
            P("pipe", None, "tensor"),
            P("pipe", None, "dp", "tensor"),
            P(None, "pipe", None, "dp", "tensor"),
            P("pipe", None, "dp", "tensor"),
            P(None, None, "dp", "tensor"),
            P(None, None, "dp", "tensor"),
        ),
        out_specs=(
            P("pipe", None, "dp", "tensor"),
            P("pipe", None, "dp", "tensor"),
            P("pipe", None, ("tensor", "dp"), None),
            P("pipe", None, "dp", "tensor"),
        ),
        check_vma=False,
    )
```

```python
import functools

import jax
import jax.numpy as jnp
from jax import lax
from jax.experimental import pallas as pl
from jax.experimental.pallas import tpu as pltpu
from jax.sharding import PartitionSpec as P

MESH = pl.DeviceIdType.MESH
EPS = 1e-06
F32 = jnp.float32
BF16 = jnp.bfloat16

FAMILIES = {
    "rs1b": 8, "rs1f": 8, "rs1h": 8, "sq1": 8, "ag1b": 8, "ds1": 8, "ag1f": 8, "ag1a": 8,
    "rs2b": 8, "rs2f": 8, "sq2": 8, "ag2b": 8, "ds2": 8, "ag2f": 8, "up": 4, "down": 4,
    "hg": 4, "dy0": 4, "dy1": 16, "a": 8, "du0": 4, "du1": 4, "mirror": 3,
}
INDEX = {}
N_SEMS = 0
for _name, _count in FAMILIES.items():
    INDEX[_name] = N_SEMS
    N_SEMS += _count


def nt(a, b):
    return lax.dot_general(a, b, (((1,), (1,)), ((), ())), preferred_element_type=F32)


def tn(a, b):
    return lax.dot_general(a, b, (((0,), (0,)), ((), ())), preferred_element_type=F32)


def nn(a, b):
    return jnp.dot(a, b, preferred_element_type=F32)


def packed(*columns):
    rows = columns[0].shape[0]
    lane = lax.broadcasted_iota(jnp.int32, (rows, 128), 1)
    row = lax.broadcasted_iota(jnp.int32, (rows, 128), 0)
    out = jnp.zeros((rows, 128), F32)
    for i, column in enumerate(columns):
        out = jnp.where(lane == row + i * rows, column, out)
    return jnp.sum(out, axis=0, keepdims=True)


def unpacked(line, rows, i):
    lane = lax.broadcasted_iota(jnp.int32, (rows, 128), 1)
    row = lax.broadcasted_iota(jnp.int32, (rows, 128), 0)
    return jnp.sum(jnp.where(lane == row + i * rows, line, 0.0), axis=1, keepdims=True)


def kernel(
    n_pipe, n_tensor, n_dp, d_model,
    wd_hbm, wu_hbm, g_hbm, x_hbm, h_hbm, dy_hbm, fresh_hbm, latest_hbm,
    y_out, dh_out, gd_out, gu_out,
    wd, wu, g, x0, h, dy0, fresh, latest, hg,
    s1b, r1b, s1f, r1f, s1h, r1h, sq1, rq1, a1b, d1, a1f, a1a,
    s2b, r2b, s2f, r2f, sq2, rq2, a2b, d2, a2f,
    ys, ds, x1, dy1, hgr, dyr, ar, dur, gd, gu, msd, msu, mrd, mru,
    in_sem, own_sem, send_sem, recv_sem, ready,
):
    p = lax.axis_index("pipe")
    t = lax.axis_index("tensor")
    k = lax.axis_index("dp")
    last = n_pipe - 1
    middle = n_pipe // 2
    slots, rows, width = x0.shape
    rank = wd.shape[2]
    half = rows // 2
    not_first, not_last = p > 0, p < last
    upper = p >= middle
    lower = p < middle
    mirror = last - p

    barrier = pltpu.get_barrier_semaphore()

    def greet(**where):
        pl.semaphore_signal(barrier, inc=1, device_id=where, device_id_type=MESH)

    @pl.when(lower)
    def _():
        greet(pipe=mirror)

    for j in range(1, n_tensor):
        greet(tensor=lax.rem(t + j, n_tensor))

    @pl.when(jnp.logical_and(not_first, p != middle))
    def _():
        greet(pipe=p - 1)

    @pl.when(not_last)
    def _():
        greet(pipe=p + 1)

    for j in range(1, n_dp):
        greet(dp=lax.rem(k + j, n_dp))

    def load(i, src, dst):
        copy = pltpu.make_async_copy(src, dst, in_sem.at[i])
        copy.start()
        return copy

    order = [lax.rem(t // 2 + i, slots) for i in (2, 1, 3, 0)]
    first = [load(0, x_hbm.at[0], x0), load(1, h_hbm.at[0, 0], h.at[0]), load(2, h_hbm.at[1, 0], h.at[1]),
             load(3, g_hbm.at[0], g)]
    by_slot = []
    for i, s in enumerate(order):
        pair = [load(4 + 2 * i, wd_hbm.at[0, s], wd.at[s]), load(5 + 2 * i, wu_hbm.at[0, s], wu.at[s])]
        if i == 0:
            pair.append(load(12, dy_hbm.at[0], dy0))
        by_slot.append(pair)
    entering = [load(13, fresh_hbm.at[0], fresh), load(14, latest_hbm.at[0], latest)]

    pending = []

    def remote(src, dst, index, **where):
        return pltpu.make_async_remote_copy(
            src_ref=src, dst_ref=dst, send_sem=send_sem.at[index], recv_sem=recv_sem.at[index],
            device_id=where, device_id_type=MESH,
        )

    ring = [4, 3, 5, 2, 6, 1, 7] if n_tensor == 8 else list(range(1, n_tensor))
    near = list(range(1, n_dp))

    class Exchange:
        def __init__(self, family, axis, src_of, dst, offset=0):
            me, count, self.steps = (t, n_tensor, ring) if axis == "tensor" else (k, n_dp, near)
            self.base, self.axis, self.src_of, self.dst = INDEX[family] + offset, axis, src_of, dst
            self.me, self.count = me, count
            pending.append(self)

        def copy(self, peer, j):
            return remote(self.src_of(peer), self.dst, self.base + j, **{self.axis: peer})

        def start_to(self, peer):
            self.copy(peer, lax.rem(peer - self.me + self.count, self.count)).start()

        def start(self):
            for j in self.steps:
                self.copy(lax.rem(self.me + j, self.count), j).start()
            return self

        def received(self):
            for j in self.steps:
                self.copy(lax.rem(self.me + j, self.count), j).wait_recv()
                yield lax.rem(self.me + self.count - j, self.count)

        def receive(self):
            for _ in self.received():
                pass

        def drain(self):
            for j in self.steps:
                self.copy(lax.rem(self.me + j, self.count), j).wait_send()

    def scatter(family, src, dst):
        return Exchange(family, "tensor", lambda peer: src.at[peer], dst.at[t])

    def gather(family, ref):
        return Exchange(family, "tensor", lambda peer: ref.at[t], ref.at[t])

    def summed(exchange, src, dst):
        total = src[t].astype(F32)
        for q in exchange.received():
            total = total + dst[q].astype(F32)
        return total

    rs1b, rs1f, rs1h = scatter("rs1b", s1b, r1b), scatter("rs1f", s1f, r1f), scatter("rs1h", s1h, r1h)
    xsq1 = scatter("sq1", sq1, rq1)
    for copy in first:
        copy.wait()
    for n, s in enumerate(order):
        gain = g[pl.ds(s, 1), :]
        xf, h0f, h1f = x0[s].astype(F32), h[0, s].astype(F32), h[1, s].astype(F32)
        h0s, h1s = (h0f * gain).astype(BF16), (h1f * gain).astype(BF16)
        hg[s, 0:rows] = h0s
        hg[s, rows : 2 * rows] = h1s
        stacked = jnp.concatenate([h0s, (xf * gain).astype(BF16), h1s], axis=0)
        for copy in by_slot[n]:
            copy.wait()
        part = nn(stacked, wd[s]).astype(BF16)
        grad = nt(dy0[s], wu[s]).astype(BF16)
        sums = [jnp.sum(v * v, axis=1, keepdims=True) for v in (xf, h0f, h1f)]
        for i in range(2):
            lo, hi = i * half, (i + 1) * half
            r = 2 * s + i
            s1b[r, :, 0:rank] = part[lo:hi]
            s1b[r, :, rank : 2 * rank] = grad[lo:hi]
            s1f[r] = part[rows + lo : rows + hi]
            s1h[r] = part[2 * rows + lo : 2 * rows + hi]
            sq1[r] = packed(*[v[lo:hi] for v in sums])
        if n == 0:
            count = n_tensor - 1 + n_dp - 1 + not_first.astype(jnp.int32) + not_last.astype(jnp.int32)
            count = count + upper.astype(jnp.int32) - (p == middle - 1).astype(jnp.int32)
            pl.semaphore_wait(barrier, count)
        for peer in ([2 * s, 2 * s + 1] if n < slots - 1 else [t + 1 - 2 * lax.rem(t, 2)]):
            xsq1.start_to(peer)
            rs1b.start_to(peer)

    @pl.when(upper)
    def _():
        pl.semaphore_signal(ready.at[0], inc=1, device_id={"pipe": mirror}, device_id_type=MESH)

    @pl.when(p == middle)
    def _():
        pl.semaphore_signal(ready.at[1], inc=1, device_id={"pipe": p - 1}, device_id_type=MESH)

    def window(peer):
        return hg.at[:, :, pl.ds(pl.multiple_of(peer * 128, 128), 256)]

    xhg = Exchange("hg", "dp", window, hgr.at[k]).start()
    xdy0 = Exchange("dy0", "dp", lambda peer: dy0, dyr.at[k, 0]).start()
    own_hg = pltpu.make_async_copy(window(k), hgr.at[k], own_sem.at[0])
    own_hg.start()
    dyr[k, 0] = dy0[...]

    @pl.when(jnp.logical_not(not_first))
    def _():
        entering[0].wait()
        entering[1].wait()
        x1[0] = fresh[0]
        dy1[1] = latest[0]

    @pl.when(jnp.logical_not(not_last))
    def _():
        entering[0].wait()
        entering[1].wait()
        x1[2] = fresh[1]
        dy1[3] = latest[1]

    @pl.when(jnp.logical_and(not_first, not_last))
    def _():
        entering[0].wait()
        entering[1].wait()

    def factor_of(column):
        return 1.0 / jnp.sqrt(column / d_model + EPS)

    def back(latent, factor, da):
        z = latent * factor
        sig = jax.nn.sigmoid(z)
        dz = da * sig * (1.0 + z * (1.0 - sig))
        dss = -0.5 * factor * factor * factor / d_model * jnp.sum(dz * latent, axis=1, keepdims=True)
        return (z * sig).astype(BF16), (dz * factor).astype(BF16), packed(dss)

    def swish(z):
        return (z * jax.nn.sigmoid(z)).astype(BF16)

    squares = summed(xsq1, sq1, rq1)
    fx, f0, f1 = (factor_of(unpacked(squares, half, i)) for i in range(3))
    total = summed(rs1b, s1b, r1b)
    ah0, du0, dss0 = back(total[:, 0:rank], f0, total[:, rank : 2 * rank])
    a1b[t] = du0
    d1[t] = dss0
    ag1b = gather("ag1b", a1b).start()
    xds1 = gather("ds1", d1).start()
    rs1f.start()
    rs1h.start()

    def both(ref, s):
        return jnp.concatenate([ref[2 * s], ref[2 * s + 1]], axis=0)

    def dh_of(a_ref, d_ref, s, kept, cot):
        dss = jnp.concatenate([unpacked(d_ref[2 * s + i], half, 0) for i in range(2)], axis=0)
        feature = nt(both(a_ref, s), wd[s]) * g[s : s + 1, :]
        return (feature + 2.0 * kept.astype(F32) * dss + cot.astype(F32)).astype(BF16)

    def y_of(a_ref, s, rows_in):
        return (rows_in.astype(F32) + nn(both(a_ref, s), wu[s])).astype(BF16)

    up_index = {("y", 0): 0, ("y", 3): 1, ("d", 1): 2, ("d", 2): 3}
    down_index = {("y", 1): 0, ("y", 2): 1, ("d", 0): 2, ("d", 3): 3}

    def shift(kind, s):
        src, dst = (ys.at[s], x1.at[s]) if kind == "y" else (ds.at[s], dy1.at[s])
        if (kind, s) in up_index:
            copy = remote(src, dst, INDEX["up"] + up_index[kind, s], pipe=p + 1)
            return not_last, not_first, copy
        copy = remote(src, dst, INDEX["down"] + down_index[kind, s], pipe=p - 1)
        return not_first, not_last, copy

    def start_shift(kind, s):
        can_send, _, copy = shift(kind, s)
        pl.when(can_send)(copy.start)

    def land(kind, s):
        _, can_receive, copy = shift(kind, s)
        pl.when(can_receive)(copy.wait_recv)

    def drain(kind, s):
        can_send, _, copy = shift(kind, s)
        pl.when(can_send)(copy.wait_send)

    ag1b.receive()
    xds1.receive()

    @pl.when(p == middle - 1)
    def _():
        pl.semaphore_wait(ready.at[1], 1)

    for s in (2, 3, 0, 1):
        ds[s] = dh_of(a1b, d1, s, h[0, s], dy0[s])
        start_shift("d", s)
    xdu0 = Exchange("du0", "dp", lambda peer: a1b, dur.at[k, 0]).start()
    dur[k, 0] = a1b[...]

    @pl.when(jnp.logical_not(not_first))
    def _():
        dy1[2] = ds[3]

    @pl.when(jnp.logical_not(not_last))
    def _():
        dy1[0] = ds[1]

    a1f[t] = swish(summed(rs1f, s1f, r1f) * fx)
    ag1f = gather("ag1f", a1f).start()
    u1 = summed(rs1h, s1h, r1h)
    a1a[t, :, 0:rank] = ah0
    a1a[t, :, rank : 2 * rank] = swish(u1 * f1)
    ag1a = gather("ag1a", a1a).start()

    rs2b, rs2f = scatter("rs2b", s2b, r2b), scatter("rs2f", s2f, r2f)
    xsq2 = scatter("sq2", sq2, rq2)
    xdy1 = []
    for s in (2, 3, 0, 1):
        land("d", s)
        grad = nt(dy1[s], wu[s]).astype(BF16)
        for i in range(2):
            r = 2 * s + i
            s2b[r] = grad[i * half : (i + 1) * half]

            @pl.when(t != r)
            def _():
                rs2b.start_to(r)

        xdy1.append(Exchange("dy1", "dp", lambda peer, s=s: dy1.at[s], dyr.at[k, 1, s], 4 * s).start())
    dyr[k, 1] = dy1[...]
    ag1f.receive()
    for s in range(slots):
        ys[s] = y_of(a1f, s, x0[s])
        start_shift("y", s)

    @pl.when(jnp.logical_not(not_first))
    def _():
        x1[3] = ys[2]

    @pl.when(jnp.logical_not(not_last))
    def _():
        x1[1] = ys[0]

    ag1a.receive()

    def latents(peer, tick):
        return a1a.at[:, :, pl.ds(pl.multiple_of(tick * rank + peer // 2 * 128, 128), 128)]

    xa = [
        Exchange("a", "dp", functools.partial(latents, tick=tick), ar.at[k, tick], 4 * tick).start()
        for tick in range(2)
    ]
    own_a = [pltpu.make_async_copy(latents(k, tick), ar.at[k, tick], own_sem.at[1 + tick]) for tick in range(2)]
    for copy in own_a:
        copy.start()

    _, du1, dss1 = back(u1, f1, summed(rs2b, s2b, r2b))
    a2b[t] = du1
    d2[t] = dss1
    ag2b = gather("ag2b", a2b).start()
    xds2 = gather("ds2", d2).start()

    for copy in own_a:
        copy.wait()
    for exchange in [xdy0] + xdy1 + xa:
        exchange.receive()

    @pl.when(lower)
    def _():
        pl.semaphore_wait(ready.at[0], 1)

    def all_rows(ref, s):
        return jnp.concatenate(
            [ref[q, tick, 2 * s + i] for q in range(n_dp) for tick in range(2) for i in range(2)], axis=0
        )

    def up_gradient(s):
        cot = jnp.concatenate([dyr[q, tick, s] for q in range(n_dp) for tick in range(2)], axis=0)
        return tn(all_rows(ar, s), cot)

    keep_up = pl.ds(pl.multiple_of(lax.rem(k, 2) * 64, 64), 64)
    for s in (2, 3):
        gu[s] = up_gradient(s)
        msu[s - 2] = gu[s, keep_up, :].astype(BF16)
    mu = remote(msu, mru, INDEX["mirror"], pipe=mirror)
    mu.start()

    for s in range(slots):
        land("y", s)
        xf = x1[s].astype(F32)
        part = nn((xf * g[s : s + 1, :]).astype(BF16), wd[s]).astype(BF16)
        squares = jnp.sum(xf * xf, axis=1, keepdims=True)
        for i in range(2):
            lo, hi = i * half, (i + 1) * half
            s2f[2 * s + i] = part[lo:hi]
            sq2[2 * s + i] = packed(squares[lo:hi])
    xsq2.start()
    rs2f.start()

    ag2b.receive()
    xds2.receive()
    xdu1 = Exchange("du1", "dp", lambda peer: a2b, dur.at[k, 1]).start()
    dur[k, 1] = a2b[...]
    own_hg.wait()
    for exchange in (xhg, xdu0, xdu1):
        exchange.receive()
    keep_down = pl.ds(pl.multiple_of(k * 32, 32), width // n_dp)

    def down_gradient(s):
        factors = jnp.concatenate([hgr[q, s] for q in range(n_dp)], axis=0)
        return tn(factors, all_rows(dur, s))

    md = []
    for s in (2, 3):
        gd[s] = down_gradient(s)
        msd[s - 2] = gd[s, keep_down, :].astype(BF16)
        md.append(remote(msd.at[s - 2], mrd.at[s - 2], INDEX["mirror"] + s - 1, pipe=mirror))
        md[-1].start()
    squares = summed(xsq2, sq2, rq2)
    a2f[t] = swish(summed(rs2f, s2f, r2f) * factor_of(unpacked(squares, half, 0)))
    ag2f = gather("ag2f", a2f).start()
    for s in (0, 1):
        gu[s] = up_gradient(s)
        gd[s] = down_gradient(s)
    for s in range(slots):
        dh_out[0, s] = dh_of(a2b, d2, s, h[1, s], dy1[s])
    ag2f.receive()
    for s in range(slots):
        y_out[0, s] = y_of(a2f, s, x1[s])
    mu.wait_recv()
    for j in range(2):
        gu_out[0, j] = gu[j, keep_up, :] + mru[j].astype(F32)
    for j in range(2):
        md[j].wait_recv()
        gd_out[0, j] = gd[j, keep_down, :] + mrd[j].astype(F32)

    for exchange in pending:
        exchange.drain()
    for copy in [mu] + md:
        copy.wait_send()
    for s in range(slots):
        drain("y", s)
        drain("d", s)


def write_kernel(*refs):
    count = len(refs) // 2
    copies = [pltpu.make_async_copy(refs[i], refs[count + i], refs[-1].at[i]) for i in range(count)]
    for copy in copies:
        copy.start()
    for copy in copies:
        copy.wait()


def solution(mesh):
    n_pipe, n_tensor, n_dp = (mesh.shape[a] for a in ("pipe", "tensor", "dp"))

    def per_device(wd, wu, g, x, h, dy, fresh, latest):
        _, slots, width, rank = wd.shape
        rows = x.shape[2]
        half = rows // 2
        chunks = n_tensor
        any_spec = pl.BlockSpec(memory_space=pl.ANY)
        vmem_spec = pl.BlockSpec(memory_space=pltpu.VMEM)
        v = pltpu.VMEM
        shapes = [
            ((1, slots, rows, width), BF16), ((1, slots, rows, width), BF16),
            ((1, 2, width // n_dp, rank), F32), ((1, 2, rank // n_dp, width), F32),
        ]

        def chunk(columns):
            return v((chunks, half, columns), BF16)

        line = v((chunks, 1, 128), F32)
        act = v((slots, rows, width), BF16)
        results = pl.pallas_call(
            functools.partial(kernel, n_pipe, n_tensor, n_dp, width * n_tensor),
            out_shape=tuple(v(*shape) for shape in shapes),
            in_specs=[any_spec] * 8,
            out_specs=(vmem_spec,) * 4,
            scratch_shapes=[
                v((slots, width, rank), BF16), v((slots, rank, width), BF16), v((slots, width), F32),
                act, v((2, slots, rows, width), BF16), act,
                v((2, rows, width), BF16), v((2, rows, width), BF16),
                v((slots, 2 * rows, width), BF16),
                chunk(2 * rank), chunk(2 * rank), chunk(rank), chunk(rank), chunk(rank), chunk(rank),
                line, line, chunk(rank), line, chunk(rank), chunk(2 * rank),
                chunk(rank), chunk(rank), chunk(rank), chunk(rank), line, line, chunk(rank), line, chunk(rank),
                act, act, act, act,
                v((n_dp, slots, 2 * rows, 256), BF16),
                v((n_dp, 2, slots, rows, width), BF16),
                v((n_dp, 2, chunks, half, 128), BF16),
                v((n_dp, 2, chunks, half, rank), BF16),
                v((slots, 256, rank), F32), v((slots, 128, width), F32),
                v((2, width // n_dp, rank), BF16), v((2, rank // n_dp, width), BF16),
                v((2, width // n_dp, rank), BF16), v((2, rank // n_dp, width), BF16),
                pltpu.SemaphoreType.DMA((15,)), pltpu.SemaphoreType.DMA((3,)),
                pltpu.SemaphoreType.DMA((N_SEMS,)), pltpu.SemaphoreType.DMA((N_SEMS,)),
                pltpu.SemaphoreType.REGULAR((2,)),
            ],
            compiler_params=pltpu.CompilerParams(
                collective_id=0, has_side_effects=True, vmem_limit_bytes=60 * 2**20
            ),
            name="relay_window",
        )(wd, wu, g, x, h, dy, fresh, latest)
        return pl.pallas_call(
            write_kernel,
            out_shape=tuple(jax.ShapeDtypeStruct(*shape) for shape in shapes),
            in_specs=[vmem_spec] * 4,
            out_specs=(any_spec,) * 4,
            scratch_shapes=[pltpu.SemaphoreType.DMA((4,))],
            name="write_results",
        )(*[pltpu.with_memory_space_constraint(r, pltpu.VMEM) for r in results])

    return jax.shard_map(
        per_device,
        mesh=mesh,
        in_specs=(
            P("pipe", None, "tensor", None),
            P("pipe", None, None, "tensor"),
            P("pipe", None, "tensor"),
            P("pipe", None, "dp", "tensor"),
            P(None, "pipe", None, "dp", "tensor"),
            P("pipe", None, "dp", "tensor"),
            P(None, None, "dp", "tensor"),
            P(None, None, "dp", "tensor"),
        ),
        out_specs=(
            P("pipe", None, "dp", "tensor"),
            P("pipe", None, "dp", "tensor"),
            P("pipe", None, ("tensor", "dp"), None),
            P("pipe", None, "dp", "tensor"),
        ),
        check_vma=False,
    )
```

```python
import functools

import jax
import jax.numpy as jnp
from jax import lax
from jax.experimental import pallas as pl
from jax.experimental.pallas import tpu as pltpu
from jax.sharding import PartitionSpec as P

MESH = pl.DeviceIdType.MESH
EPS = 1e-06
F32 = jnp.float32
BF16 = jnp.bfloat16

FAMILIES = {
    "rs1b": 8, "rs1f": 8, "rs1h": 8, "sq1": 8, "ag1b": 8, "ds1": 8, "ag1f": 8, "ag1a": 8,
    "rs2b": 8, "rs2f": 8, "sq2": 8, "ag2b": 8, "ds2": 8, "ag2f": 8, "up": 4, "down": 4,
    "hg": 4, "dy0": 4, "dy1": 16, "a": 16, "du0": 4, "du1": 4, "mirror": 3,
}
INDEX = {}
N_SEMS = 0
for _name, _count in FAMILIES.items():
    INDEX[_name] = N_SEMS
    N_SEMS += _count


def nt(a, b):
    return lax.dot_general(a, b, (((1,), (1,)), ((), ())), preferred_element_type=F32)


def tn(a, b):
    return lax.dot_general(a, b, (((0,), (0,)), ((), ())), preferred_element_type=F32)


def nn(a, b):
    return jnp.dot(a, b, preferred_element_type=F32)


def packed(*columns):
    rows = columns[0].shape[0]
    lane = lax.broadcasted_iota(jnp.int32, (rows, 128), 1)
    row = lax.broadcasted_iota(jnp.int32, (rows, 128), 0)
    out = jnp.zeros((rows, 128), F32)
    for i, column in enumerate(columns):
        out = jnp.where(lane == row + i * rows, column, out)
    return jnp.sum(out, axis=0, keepdims=True)


def unpacked(line, rows, i):
    lane = lax.broadcasted_iota(jnp.int32, (rows, 128), 1)
    row = lax.broadcasted_iota(jnp.int32, (rows, 128), 0)
    return jnp.sum(jnp.where(lane == row + i * rows, line, 0.0), axis=1, keepdims=True)


def kernel(
    n_pipe, n_tensor, n_dp, d_model,
    wd_hbm, wu_hbm, g_hbm, x_hbm, h_hbm, dy_hbm, fresh_hbm, latest_hbm,
    y_out, dh_out, gd_out, gu_out,
    wd, wu, g, x0, h, dy0, fresh, latest, hg,
    s1b, r1b, s1f, r1f, s1h, r1h, sq1, rq1, a1b, d1, a1f, a1a,
    s2b, r2b, s2f, r2f, sq2, rq2, a2b, d2, a2f,
    ys, ds, x1, dy1, hgr, dyr, ar, dur, gd, gu, msd, msu, mrd, mru,
    in_sem, own_sem, send_sem, recv_sem, ready,
):
    p = lax.axis_index("pipe")
    t = lax.axis_index("tensor")
    k = lax.axis_index("dp")
    last = n_pipe - 1
    middle = n_pipe // 2
    slots, rows, width = x0.shape
    rank = wd.shape[2]
    half = rows // 2
    not_first, not_last = p > 0, p < last
    upper = p >= middle
    lower = p < middle
    mirror = last - p

    barrier = pltpu.get_barrier_semaphore()

    def greet(**where):
        pl.semaphore_signal(barrier, inc=1, device_id=where, device_id_type=MESH)

    @pl.when(lower)
    def _():
        greet(pipe=mirror)

    for j in range(1, n_tensor):
        greet(tensor=lax.rem(t + j, n_tensor))

    @pl.when(jnp.logical_and(not_first, p != middle))
    def _():
        greet(pipe=p - 1)

    @pl.when(not_last)
    def _():
        greet(pipe=p + 1)

    for j in range(1, n_dp):
        greet(dp=lax.rem(k + j, n_dp))

    def load(i, src, dst):
        copy = pltpu.make_async_copy(src, dst, in_sem.at[i])
        copy.start()
        return copy

    order = [lax.rem(t // 2 + i, slots) for i in (2, 1, 3, 0)]
    first = [load(0, x_hbm.at[0], x0), load(1, h_hbm.at[0, 0], h.at[0]), load(2, h_hbm.at[1, 0], h.at[1]),
             load(3, g_hbm.at[0], g)]
    by_slot = []
    for i, s in enumerate(order):
        pair = [load(4 + 2 * i, wd_hbm.at[0, s], wd.at[s]), load(5 + 2 * i, wu_hbm.at[0, s], wu.at[s])]
        if i == 0:
            pair.append(load(12, dy_hbm.at[0], dy0))
        by_slot.append(pair)
    entering = [load(13, fresh_hbm.at[0], fresh), load(14, latest_hbm.at[0], latest)]

    pending = []

    def remote(src, dst, index, **where):
        return pltpu.make_async_remote_copy(
            src_ref=src, dst_ref=dst, send_sem=send_sem.at[index], recv_sem=recv_sem.at[index],
            device_id=where, device_id_type=MESH,
        )

    ring = [4, 3, 5, 2, 6, 1, 7] if n_tensor == 8 else list(range(1, n_tensor))
    near = list(range(1, n_dp))

    class Exchange:
        def __init__(self, family, axis, src_of, dst, offset=0):
            me, count, self.steps = (t, n_tensor, ring) if axis == "tensor" else (k, n_dp, near)
            self.base, self.axis, self.src_of, self.dst = INDEX[family] + offset, axis, src_of, dst
            self.me, self.count = me, count
            pending.append(self)

        def copy(self, peer, j):
            return remote(self.src_of(peer), self.dst, self.base + j, **{self.axis: peer})

        def start_to(self, peer):
            self.copy(peer, lax.rem(peer - self.me + self.count, self.count)).start()

        def start(self):
            for j in self.steps:
                self.copy(lax.rem(self.me + j, self.count), j).start()
            return self

        def received(self):
            for j in self.steps:
                self.copy(lax.rem(self.me + j, self.count), j).wait_recv()
                yield lax.rem(self.me + self.count - j, self.count)

        def receive(self):
            for _ in self.received():
                pass

        def drain(self):
            for j in self.steps:
                self.copy(lax.rem(self.me + j, self.count), j).wait_send()

    def scatter(family, src, dst):
        return Exchange(family, "tensor", lambda peer: src.at[peer], dst.at[t])

    def gather(family, ref):
        return Exchange(family, "tensor", lambda peer: ref.at[t], ref.at[t])

    def summed(exchange, src, dst):
        total = src[t].astype(F32)
        for q in exchange.received():
            total = total + dst[q].astype(F32)
        return total

    rs1b, rs1f, rs1h = scatter("rs1b", s1b, r1b), scatter("rs1f", s1f, r1f), scatter("rs1h", s1h, r1h)
    xsq1 = scatter("sq1", sq1, rq1)
    for copy in first:
        copy.wait()
    for n, s in enumerate(order):
        gain = g[pl.ds(s, 1), :]
        xf, h0f, h1f = x0[s].astype(F32), h[0, s].astype(F32), h[1, s].astype(F32)
        h0s, h1s = (h0f * gain).astype(BF16), (h1f * gain).astype(BF16)
        hg[s, 0:rows] = h0s
        hg[s, rows : 2 * rows] = h1s
        stacked = jnp.concatenate([h0s, (xf * gain).astype(BF16), h1s], axis=0)
        for copy in by_slot[n]:
            copy.wait()
        part = nn(stacked, wd[s]).astype(BF16)
        grad = nt(dy0[s], wu[s]).astype(BF16)
        sums = [jnp.sum(v * v, axis=1, keepdims=True) for v in (xf, h0f, h1f)]
        for i in range(2):
            lo, hi = i * half, (i + 1) * half
            r = 2 * s + i
            s1b[r, :, 0:rank] = part[lo:hi]
            s1b[r, :, rank : 2 * rank] = grad[lo:hi]
            s1f[r] = part[rows + lo : rows + hi]
            s1h[r] = part[2 * rows + lo : 2 * rows + hi]
            sq1[r] = packed(*[v[lo:hi] for v in sums])
        if n == 0:
            count = n_tensor - 1 + n_dp - 1 + not_first.astype(jnp.int32) + not_last.astype(jnp.int32)
            count = count + upper.astype(jnp.int32) - (p == middle - 1).astype(jnp.int32)
            pl.semaphore_wait(barrier, count)
        for peer in ([2 * s, 2 * s + 1] if n < slots - 1 else [t + 1 - 2 * lax.rem(t, 2)]):
            xsq1.start_to(peer)
            rs1b.start_to(peer)

    @pl.when(upper)
    def _():
        pl.semaphore_signal(ready.at[0], inc=1, device_id={"pipe": mirror}, device_id_type=MESH)

    @pl.when(p == middle)
    def _():
        pl.semaphore_signal(ready.at[1], inc=1, device_id={"pipe": p - 1}, device_id_type=MESH)

    def window(peer):
        return hg.at[:, :, pl.ds(pl.multiple_of(peer * 128, 128), 256)]

    xhg = Exchange("hg", "dp", window, hgr.at[k]).start()
    xdy0 = Exchange("dy0", "dp", lambda peer: dy0, dyr.at[k, 0]).start()
    own_hg = pltpu.make_async_copy(window(k), hgr.at[k], own_sem.at[0])
    own_hg.start()
    dyr[k, 0] = dy0[...]

    @pl.when(jnp.logical_not(not_first))
    def _():
        entering[0].wait()
        entering[1].wait()
        x1[0] = fresh[0]
        dy1[1] = latest[0]

    @pl.when(jnp.logical_not(not_last))
    def _():
        entering[0].wait()
        entering[1].wait()
        x1[2] = fresh[1]
        dy1[3] = latest[1]

    @pl.when(jnp.logical_and(not_first, not_last))
    def _():
        entering[0].wait()
        entering[1].wait()

    def factor_of(column):
        return 1.0 / jnp.sqrt(column / d_model + EPS)

    def back(latent, factor, da):
        z = latent * factor
        sig = jax.nn.sigmoid(z)
        dz = da * sig * (1.0 + z * (1.0 - sig))
        dss = -0.5 * factor * factor * factor / d_model * jnp.sum(dz * latent, axis=1, keepdims=True)
        return (z * sig).astype(BF16), (dz * factor).astype(BF16), packed(dss)

    def swish(z):
        return (z * jax.nn.sigmoid(z)).astype(BF16)

    squares = summed(xsq1, sq1, rq1)
    fx, f0, f1 = (factor_of(unpacked(squares, half, i)) for i in range(3))
    total = summed(rs1b, s1b, r1b)
    ah0, du0, dss0 = back(total[:, 0:rank], f0, total[:, rank : 2 * rank])
    a1b[t] = du0
    d1[t] = dss0
    ag1b = gather("ag1b", a1b).start()
    xds1 = gather("ds1", d1).start()
    rs1f.start()
    rs1h.start()

    def both(ref, s):
        return jnp.concatenate([ref[2 * s], ref[2 * s + 1]], axis=0)

    def dh_of(a_ref, d_ref, s, kept, cot):
        dss = jnp.concatenate([unpacked(d_ref[2 * s + i], half, 0) for i in range(2)], axis=0)
        feature = nt(both(a_ref, s), wd[s]) * g[s : s + 1, :]
        return (feature + 2.0 * kept.astype(F32) * dss + cot.astype(F32)).astype(BF16)

    def y_of(a_ref, s, rows_in):
        return (rows_in.astype(F32) + nn(both(a_ref, s), wu[s])).astype(BF16)

    up_index = {("y", 0): 0, ("y", 3): 1, ("d", 1): 2, ("d", 2): 3}
    down_index = {("y", 1): 0, ("y", 2): 1, ("d", 0): 2, ("d", 3): 3}

    def shift(kind, s):
        src, dst = (ys.at[s], x1.at[s]) if kind == "y" else (ds.at[s], dy1.at[s])
        if (kind, s) in up_index:
            copy = remote(src, dst, INDEX["up"] + up_index[kind, s], pipe=p + 1)
            return not_last, not_first, copy
        copy = remote(src, dst, INDEX["down"] + down_index[kind, s], pipe=p - 1)
        return not_first, not_last, copy

    def start_shift(kind, s):
        can_send, _, copy = shift(kind, s)
        pl.when(can_send)(copy.start)

    def land(kind, s):
        _, can_receive, copy = shift(kind, s)
        pl.when(can_receive)(copy.wait_recv)

    def drain(kind, s):
        can_send, _, copy = shift(kind, s)
        pl.when(can_send)(copy.wait_send)

    ag1b.receive()
    xds1.receive()

    @pl.when(p == middle - 1)
    def _():
        pl.semaphore_wait(ready.at[1], 1)

    for s in (2, 3, 0, 1):
        ds[s] = dh_of(a1b, d1, s, h[0, s], dy0[s])
        start_shift("d", s)
    xdu0 = Exchange("du0", "dp", lambda peer: a1b, dur.at[k, 0]).start()
    dur[k, 0] = a1b[...]

    @pl.when(jnp.logical_not(not_first))
    def _():
        dy1[2] = ds[3]

    @pl.when(jnp.logical_not(not_last))
    def _():
        dy1[0] = ds[1]

    a1f[t] = swish(summed(rs1f, s1f, r1f) * fx)
    ag1f = gather("ag1f", a1f).start()
    u1 = summed(rs1h, s1h, r1h)
    a1a[t, :, 0:rank] = ah0
    a1a[t, :, rank : 2 * rank] = swish(u1 * f1)
    ag1a = gather("ag1a", a1a).start()

    rs2b, rs2f = scatter("rs2b", s2b, r2b), scatter("rs2f", s2f, r2f)
    xsq2 = scatter("sq2", sq2, rq2)
    xdy1 = []
    for s in (2, 3, 0, 1):
        land("d", s)
        grad = nt(dy1[s], wu[s]).astype(BF16)
        for i in range(2):
            r = 2 * s + i
            s2b[r] = grad[i * half : (i + 1) * half]

            @pl.when(t != r)
            def _():
                rs2b.start_to(r)

        xdy1.append(Exchange("dy1", "dp", lambda peer, s=s: dy1.at[s], dyr.at[k, 1, s], 4 * s))
        if s >= 2:
            xdy1[-1].start()
    dyr[k, 1] = dy1[...]
    ag1f.receive()
    for s in range(slots):
        ys[s] = y_of(a1f, s, x0[s])
        start_shift("y", s)

    @pl.when(jnp.logical_not(not_first))
    def _():
        x1[3] = ys[2]

    @pl.when(jnp.logical_not(not_last))
    def _():
        x1[1] = ys[0]

    ag1a.receive()

    def latents(peer, tick, part=pl.ds(0, n_tensor)):
        return a1a.at[part, :, pl.ds(pl.multiple_of(tick * rank + peer // 2 * 128, 128), 128)]

    xa = [
        [
            Exchange("a", "dp", functools.partial(latents, tick=tick, part=part), ar.at[k, tick, part], 8 * i + 4 * tick).start()
            for tick in range(2)
        ]
        for i, part in enumerate([pl.ds(n_tensor // 2, n_tensor // 2), pl.ds(0, n_tensor // 2)])
    ]
    for exchange in xdy1[2:]:
        exchange.start()
    own_a = [pltpu.make_async_copy(latents(k, tick), ar.at[k, tick], own_sem.at[1 + tick]) for tick in range(2)]
    for copy in own_a:
        copy.start()

    _, du1, dss1 = back(u1, f1, summed(rs2b, s2b, r2b))
    a2b[t] = du1
    d2[t] = dss1
    ag2b = gather("ag2b", a2b).start()
    xds2 = gather("ds2", d2).start()

    for copy in own_a:
        copy.wait()
    for exchange in [xdy0] + xdy1[:2] + xa[0]:
        exchange.receive()

    @pl.when(lower)
    def _():
        pl.semaphore_wait(ready.at[0], 1)

    def all_rows(ref, s):
        return jnp.concatenate(
            [ref[q, tick, 2 * s + i] for q in range(n_dp) for tick in range(2) for i in range(2)], axis=0
        )

    def up_gradient(s):
        cot = jnp.concatenate([dyr[q, tick, s] for q in range(n_dp) for tick in range(2)], axis=0)
        return tn(all_rows(ar, s), cot)

    keep_up = pl.ds(pl.multiple_of(lax.rem(k, 2) * 64, 64), 64)
    for s in (2, 3):
        gu[s] = up_gradient(s)
        msu[s - 2] = gu[s, keep_up, :].astype(BF16)
    mu = remote(msu, mru, INDEX["mirror"], pipe=mirror)
    mu.start()

    for s in range(slots):
        land("y", s)
        xf = x1[s].astype(F32)
        part = nn((xf * g[s : s + 1, :]).astype(BF16), wd[s]).astype(BF16)
        squares = jnp.sum(xf * xf, axis=1, keepdims=True)
        for i in range(2):
            lo, hi = i * half, (i + 1) * half
            s2f[2 * s + i] = part[lo:hi]
            sq2[2 * s + i] = packed(squares[lo:hi])
    xsq2.start()
    rs2f.start()

    ag2b.receive()
    xds2.receive()
    xdu1 = Exchange("du1", "dp", lambda peer: a2b, dur.at[k, 1]).start()
    dur[k, 1] = a2b[...]
    own_hg.wait()
    for exchange in (xhg, xdu0, xdu1):
        exchange.receive()
    keep_down = pl.ds(pl.multiple_of(k * 32, 32), width // n_dp)

    def down_gradient(s):
        factors = jnp.concatenate([hgr[q, s] for q in range(n_dp)], axis=0)
        return tn(factors, all_rows(dur, s))

    md = []
    for s in (2, 3):
        gd[s] = down_gradient(s)
        msd[s - 2] = gd[s, keep_down, :].astype(BF16)
        md.append(remote(msd.at[s - 2], mrd.at[s - 2], INDEX["mirror"] + s - 1, pipe=mirror))
        md[-1].start()
    squares = summed(xsq2, sq2, rq2)
    a2f[t] = swish(summed(rs2f, s2f, r2f) * factor_of(unpacked(squares, half, 0)))
    ag2f = gather("ag2f", a2f).start()
    for exchange in xdy1[2:] + xa[1]:
        exchange.receive()
    for s in (0, 1):
        gu[s] = up_gradient(s)
        gd[s] = down_gradient(s)
    for s in range(slots):
        dh_out[0, s] = dh_of(a2b, d2, s, h[1, s], dy1[s])
    ag2f.receive()
    for s in range(slots):
        y_out[0, s] = y_of(a2f, s, x1[s])
    mu.wait_recv()
    for j in range(2):
        gu_out[0, j] = gu[j, keep_up, :] + mru[j].astype(F32)
    for j in range(2):
        md[j].wait_recv()
        gd_out[0, j] = gd[j, keep_down, :] + mrd[j].astype(F32)

    for exchange in pending:
        exchange.drain()
    for copy in [mu] + md:
        copy.wait_send()
    for s in range(slots):
        drain("y", s)
        drain("d", s)


def write_kernel(*refs):
    count = len(refs) // 2
    copies = [pltpu.make_async_copy(refs[i], refs[count + i], refs[-1].at[i]) for i in range(count)]
    for copy in copies:
        copy.start()
    for copy in copies:
        copy.wait()


def solution(mesh):
    n_pipe, n_tensor, n_dp = (mesh.shape[a] for a in ("pipe", "tensor", "dp"))

    def per_device(wd, wu, g, x, h, dy, fresh, latest):
        _, slots, width, rank = wd.shape
        rows = x.shape[2]
        half = rows // 2
        chunks = n_tensor
        any_spec = pl.BlockSpec(memory_space=pl.ANY)
        vmem_spec = pl.BlockSpec(memory_space=pltpu.VMEM)
        v = pltpu.VMEM
        shapes = [
            ((1, slots, rows, width), BF16), ((1, slots, rows, width), BF16),
            ((1, 2, width // n_dp, rank), F32), ((1, 2, rank // n_dp, width), F32),
        ]

        def chunk(columns):
            return v((chunks, half, columns), BF16)

        line = v((chunks, 1, 128), F32)
        act = v((slots, rows, width), BF16)
        results = pl.pallas_call(
            functools.partial(kernel, n_pipe, n_tensor, n_dp, width * n_tensor),
            out_shape=tuple(v(*shape) for shape in shapes),
            in_specs=[any_spec] * 8,
            out_specs=(vmem_spec,) * 4,
            scratch_shapes=[
                v((slots, width, rank), BF16), v((slots, rank, width), BF16), v((slots, width), F32),
                act, v((2, slots, rows, width), BF16), act,
                v((2, rows, width), BF16), v((2, rows, width), BF16),
                v((slots, 2 * rows, width), BF16),
                chunk(2 * rank), chunk(2 * rank), chunk(rank), chunk(rank), chunk(rank), chunk(rank),
                line, line, chunk(rank), line, chunk(rank), chunk(2 * rank),
                chunk(rank), chunk(rank), chunk(rank), chunk(rank), line, line, chunk(rank), line, chunk(rank),
                act, act, act, act,
                v((n_dp, slots, 2 * rows, 256), BF16),
                v((n_dp, 2, slots, rows, width), BF16),
                v((n_dp, 2, chunks, half, 128), BF16),
                v((n_dp, 2, chunks, half, rank), BF16),
                v((slots, 256, rank), F32), v((slots, 128, width), F32),
                v((2, width // n_dp, rank), BF16), v((2, rank // n_dp, width), BF16),
                v((2, width // n_dp, rank), BF16), v((2, rank // n_dp, width), BF16),
                pltpu.SemaphoreType.DMA((15,)), pltpu.SemaphoreType.DMA((3,)),
                pltpu.SemaphoreType.DMA((N_SEMS,)), pltpu.SemaphoreType.DMA((N_SEMS,)),
                pltpu.SemaphoreType.REGULAR((2,)),
            ],
            compiler_params=pltpu.CompilerParams(
                collective_id=0, has_side_effects=True, vmem_limit_bytes=60 * 2**20
            ),
            name="relay_window",
        )(wd, wu, g, x, h, dy, fresh, latest)
        return pl.pallas_call(
            write_kernel,
            out_shape=tuple(jax.ShapeDtypeStruct(*shape) for shape in shapes),
            in_specs=[vmem_spec] * 4,
            out_specs=(any_spec,) * 4,
            scratch_shapes=[pltpu.SemaphoreType.DMA((4,))],
            name="write_results",
        )(*[pltpu.with_memory_space_constraint(r, pltpu.VMEM) for r in results])

    return jax.shard_map(
        per_device,
        mesh=mesh,
        in_specs=(
            P("pipe", None, "tensor", None),
            P("pipe", None, None, "tensor"),
            P("pipe", None, "tensor"),
            P("pipe", None, "dp", "tensor"),
            P(None, "pipe", None, "dp", "tensor"),
            P("pipe", None, "dp", "tensor"),
            P(None, None, "dp", "tensor"),
            P(None, None, "dp", "tensor"),
        ),
        out_specs=(
            P("pipe", None, "dp", "tensor"),
            P("pipe", None, "dp", "tensor"),
            P("pipe", None, ("tensor", "dp"), None),
            P("pipe", None, "dp", "tensor"),
        ),
        check_vma=False,
    )
```
